256 devices in a mesh: row: 64 (over y_lo, x, z), col: 4 (over y_hi, core).
Axes of the slice: x: 4, y: 4 (y_hi: 2, y_lo: 2; y = y_hi * 2 + y_lo), z: 8, core: 2. Of those that a mesh axis runs over, the one named last changes fastest.
Arguments:
- amplitudes: float32 [4096, 2048], P(('row', 'col')), may hold values from -6 to 6
- integrals: float32 [2048, 89600], P('col', 'row'), may hold values from -0.125 to 0.125
Outputs:
- ladder: float32 [4096, 89600], P(('row', 'col'))
The draws below stay inside these ranges and needn't reach their ends.
All inputs are finite; a program needn't handle non-finite values.
Results may differ from the reference program's by a relative error of at most 0.000071.
Values sent between devices are 32-bit elements; how exact they have to be, the bound alone decides.
No kernel may reach another device: no remote copies, remote signals or barrier semaphores. Data moves between devices by JAX's collectives and lax.ppermute only.
A program may use at most 128 MiB of HBM per device.

```python
import jax
import jax.numpy as jnp
from jax import lax

CONTRACT = 2048
PAIRS = 4096
COLUMNS = 89600


def level_of(stream_key, extent, cuts, least, largest):
    factor_of = 1.0
    for position, shards_of in cuts:
        draws = jax.random.uniform(jax.random.fold_in(jax.random.fold_in(stream_key, 6), position), (shards_of,), jnp.float32, least / len(cuts), largest / len(cuts))
        factor_of = factor_of * jnp.repeat(jnp.exp(draws), extent[position] // shards_of).reshape((-1,) + (1,) * (len(extent) - 1 - position))
    return factor_of


def bell_draw(own_key, shape, deviation, reach, split=(), held_as=jnp.bfloat16):
    entries = deviation * jax.random.normal(own_key, shape, jnp.float32)
    if split:
        entries = entries * level_of(own_key, shape, split, -0.22, 0.18)
    return jnp.clip(entries, -reach, reach).astype(held_as)


def setup_inputs(seed: int = 0) -> dict:
    seeds = jax.random.split(jax.random.key(seed), 3)
    return {
        "amplitudes": bell_draw(seeds[0], (PAIRS, CONTRACT), 1.0, 6.0, ((0, 256),), jnp.float32),
        "integrals": bell_draw(seeds[1], (CONTRACT, COLUMNS), CONTRACT ** -0.5, 0.125, ((0, 4), (1, 64)), jnp.float32),
    }


def reference(amplitudes, integrals):
    ladder_sum = jnp.dot(amplitudes, integrals, precision=lax.Precision.HIGHEST, preferred_element_type=jnp.float32)
    return 0.5 * ladder_sum
```

```python
import functools

import jax
import jax.numpy as jnp
from jax import lax
from jax.experimental import pallas as pl
from jax.experimental.pallas import tpu as pltpu
from jax.sharding import Mesh, PartitionSpec as P

AXES = ("yl", "x", "z", "yh", "core")
TILE = 256
SPLIT = 3
GROUP = 16


def swap_core(value):
    return lax.ppermute(value, "core", [(0, 1), (1, 0)])


def swap_near(value):
    return lax.ppermute(value, "yl", [(0, 1), (1, 0)])


def swap_far(value):
    return lax.ppermute(value, ("yl", "yh"), [(2, 1), (1, 2), (3, 0), (0, 3)])


def halves(value):
    top = value.astype(jnp.bfloat16)
    rest = (value - top.astype(jnp.float32)).astype(jnp.bfloat16)
    return top, rest


def split_kernel(own_ref, t_ref, top_ref, rest_ref):
    part = t_ref.shape[1] // 4
    for q in range(4):
        source = pl.multiple_of((own_ref[0] ^ q) * part, part)
        depth = pl.ds(q * part, part)
        top_ref[:, depth], rest_ref[:, depth] = halves(t_ref[:, pl.ds(source, part)])


def split(own, t):
    rows, depth = t.shape
    block = min(rows, 128)
    spec = pl.BlockSpec((block, depth), lambda r, own: (r, 0))
    return pl.pallas_call(
        split_kernel,
        grid_spec=pltpu.PrefetchScalarGridSpec(
            num_scalar_prefetch=1, grid=(rows // block,), in_specs=[spec], out_specs=[spec] * 2
        ),
        out_shape=[jax.ShapeDtypeStruct((rows, depth), jnp.bfloat16)] * 2,
        cost_estimate=pl.CostEstimate(
            flops=4 * rows * depth, bytes_accessed=8 * rows * depth, transcendentals=0
        ),
    )(own, t)


def product_kernel(counts, top_ref, rest_ref, *refs):
    pieces, out_ref = refs[:-1], refs[-1]
    dot = functools.partial(
        lax.dot_general,
        dimension_numbers=(((1,), (1,)), ((), ())),
        preferred_element_type=jnp.float32,
    )
    total, at = None, 0
    for q, count in enumerate(counts):
        value = pieces[at][...]
        if count == 2:
            value = jnp.where(pl.program_id(0) < SPLIT, value, pieces[at + 1][...])
        at += count
        top, rest = halves(value)
        depth = pl.ds(q * value.shape[1], value.shape[1])
        t_top, t_rest = top_ref[:, depth], rest_ref[:, depth]
        term = dot(t_top, rest) + dot(t_rest, top) + dot(t_top, top)
        total = term if total is None else total + term
    out_ref[...] = 0.5 * total


def product(t_top, t_rest, quarters, columns):
    rows, depth = t_top.shape
    part = depth // 4
    whole = pl.BlockSpec((rows, depth), lambda n: (0, 0), pipeline_mode=pl.Buffered(1))
    specs, pieces = [], []
    for quarter in quarters:
        if len(quarter) == 1:
            specs += [pl.BlockSpec((TILE, part), lambda n: (n, 0))]
        else:
            specs += [
                pl.BlockSpec((TILE, part), lambda n: (jnp.minimum(n, SPLIT - 1), 0)),
                pl.BlockSpec((TILE, part), lambda n: (jnp.maximum(n - SPLIT, 0), 0)),
            ]
        pieces += quarter
    return pl.pallas_call(
        functools.partial(product_kernel, [len(quarter) for quarter in quarters]),
        grid=(pl.cdiv(columns, TILE),),
        in_specs=[whole] * 2 + specs,
        out_specs=pl.BlockSpec((rows, TILE), lambda n: (0, n)),
        out_shape=jax.ShapeDtypeStruct((rows, columns), jnp.float32),
        compiler_params=pltpu.CompilerParams(vmem_limit_bytes=32 << 20),
        cost_estimate=pl.CostEstimate(
            flops=6 * rows * depth * columns,
            bytes_accessed=4 * (rows * depth + depth * columns + rows * columns),
            transcendentals=0,
        ),
    )(t_top, t_rest, *pieces)


def place_kernel(at_ref, block_ref, *refs):
    out_ref = refs[-1]
    width = block_ref.shape[2]
    for s in range(GROUP):
        out_ref[:, s * width : (s + 1) * width] = block_ref[s]


def place(at, block, out=None):
    sources, rows, width = block.shape
    steps = sources // GROUP
    return pl.pallas_call(
        place_kernel,
        grid_spec=pltpu.PrefetchScalarGridSpec(
            num_scalar_prefetch=1,
            grid=(steps,),
            in_specs=[pl.BlockSpec((GROUP, rows, width), lambda g, at: (g, 0, 0))]
            + ([] if out is None else [pl.BlockSpec(memory_space=pl.ANY)]),
            out_specs=pl.BlockSpec((rows, GROUP * width), lambda g, at: (0, at[0] * steps + g)),
        ),
        out_shape=jax.ShapeDtypeStruct((rows, 2 * sources * width), jnp.float32),
        input_output_aliases={} if out is None else {2: 0},
        compiler_params=pltpu.CompilerParams(vmem_limit_bytes=16 << 20),
        cost_estimate=pl.CostEstimate(
            flops=0, bytes_accessed=8 * sources * rows * width, transcendentals=0
        ),
    )(at, block, *([] if out is None else [out]))


def on_device(amplitudes, integrals):
    yl, yh, core = (lax.axis_index(name) for name in ("yl", "yh", "core"))
    rows = amplitudes.shape[0]
    columns = integrals.shape[1]
    t = lax.all_gather(amplitudes, ("x", "z"), axis=0, tiled=True)
    t_top, t_rest = split((2 * yh + core).reshape(1), t)

    own = integrals.T
    near, far = swap_near(own), swap_far(own)
    cut = SPLIT * TILE
    across = [swap_far(near[:cut]), swap_near(far[cut:])]
    own2, near2, far2 = swap_core(own), swap_core(near), swap_core(far)
    across2 = [swap_core(v) for v in across]

    def exchange(v):
        return lax.all_to_all(
            v.reshape(-1, rows, columns), ("x", "z"), split_axis=0, concat_axis=0, tiled=True
        )

    other_block = exchange(product(t_top, t_rest, [[near], [near2], [far], [far2]], columns))
    own_block = exchange(product(t_top, t_rest, [[own], [own2], across, across2], columns))
    out = place((1 - yl).reshape(1), other_block)
    return place(yl.reshape(1), own_block, out)


def solution(mesh):
    grid = Mesh(mesh.devices.reshape(2, 4, 8, 2, 2), AXES)
    return jax.shard_map(
        on_device,
        mesh=grid,
        in_specs=(P(AXES, None), P(("yh", "core"), ("yl", "x", "z"))),
        out_specs=P(AXES, None),
        check_vma=False,
    )
```

```python
import functools
import math

import jax
import jax.numpy as jnp
from jax import lax
from jax.experimental import pallas as pl
from jax.experimental.pallas import tpu as pltpu
from jax.sharding import Mesh, PartitionSpec as P

AXES = ("yl", "x", "z", "yh", "core")
TILE = 256
CUT = 768
GROUP = 16


def swap_core(value):
    return lax.ppermute(value, "core", [(0, 1), (1, 0)])


def shift_x(value, by):
    return lax.ppermute(value, "x", [(i, (i + by) % 4) for i in range(4)])


def swap_near(value):
    return lax.ppermute(value, "yl", [(0, 1), (1, 0)])


def swap_far(value):
    return lax.ppermute(value, ("yl", "yh"), [(2, 1), (1, 2), (3, 0), (0, 3)])


def halves(value):
    top = value.astype(jnp.bfloat16)
    rest = (value - top.astype(jnp.float32)).astype(jnp.bfloat16)
    return top, rest


def load_amplitudes(place_ref, pieces, last_ref, top_ref, rest_ref):
    own, x = place_ref[0], place_ref[1]
    part = last_ref.shape[3]

    @pl.loop(0, 4)
    def _(q):
        source = own ^ q
        take = pl.ds(pl.multiple_of(jnp.minimum(source, 2) * part, part), part)
        into = pl.ds(pl.multiple_of(q * part, part), part)
        for d, refs in enumerate(pieces):
            last = last_ref[:, d].reshape(-1, part)
            row = lax.rem(x + d, 4) * last.shape[0]
            at = 0
            for ref in refs:
                count = ref.shape[0]
                value = jnp.where(source < 3, ref[:, take], last[at : at + count])
                rows = pl.ds(pl.multiple_of(row + at, count), count)
                top_ref[rows, into], rest_ref[rows, into] = halves(value)
                at += count


def product_kernel(counts, place_ref, *refs):
    pieces, (out_ref, top_ref, rest_ref) = refs[6:-3], refs[-3:]

    @pl.when(pl.program_id(0) == 0)
    def _():
        here, ahead, behind, low, high, last_ref = refs[:6]
        load_amplitudes(
            place_ref, [[here], [ahead], [low, high], [behind]], last_ref, top_ref, rest_ref
        )

    dot = functools.partial(
        lax.dot_general,
        dimension_numbers=(((1,), (1,)), ((), ())),
        preferred_element_type=jnp.float32,
    )
    total, at = None, 0
    for q, tiles in enumerate(counts):
        value, start = pieces[at][...], tiles[0]
        for i, count in enumerate(tiles[1:]):
            value = jnp.where(pl.program_id(0) < start, value, pieces[at + 1 + i][...])
            start += count
        at += len(tiles)
        top, rest = halves(value)
        depth = pl.ds(q * value.shape[1], value.shape[1])
        t_top, t_rest = top_ref[:, depth], rest_ref[:, depth]
        term = dot(t_top, rest) + dot(t_rest, top) + dot(t_top, top)
        total = term if total is None else total + term
    out_ref[...] = 0.5 * total


def product(place, amplitudes, quarters):
    last = amplitudes[-1]
    rows, part = math.prod(last.shape[:3]), last.shape[3]
    depth = 4 * part
    columns = sum(piece.shape[0] for piece in quarters[0])
    specs, counts = [], []
    for quarter in quarters:
        start, tiles = 0, []
        for piece in quarter:
            count = pl.cdiv(piece.shape[0], TILE)
            specs.append(
                pl.BlockSpec(
                    (TILE, part),
                    lambda n, place, start=start, count=count: (jnp.clip(n - start, 0, count - 1), 0),
                )
            )
            tiles.append(count)
            start += count
        counts.append(tiles)
    whole = [
        pl.BlockSpec(v.shape, lambda n, place, v=v: (0,) * v.ndim, pipeline_mode=pl.Buffered(1))
        for v in amplitudes
    ]
    return pl.pallas_call(
        functools.partial(product_kernel, counts),
        grid_spec=pltpu.PrefetchScalarGridSpec(
            num_scalar_prefetch=1,
            grid=(pl.cdiv(columns, TILE),),
            in_specs=whole + specs,
            out_specs=pl.BlockSpec((rows, TILE), lambda n, place: (0, n)),
            scratch_shapes=[pltpu.VMEM((rows, depth), jnp.bfloat16)] * 2,
        ),
        out_shape=jax.ShapeDtypeStruct((rows, columns), jnp.float32),
        compiler_params=pltpu.CompilerParams(vmem_limit_bytes=60 << 20),
        cost_estimate=pl.CostEstimate(
            flops=6 * rows * depth * columns,
            bytes_accessed=4 * (rows * depth + depth * columns + rows * columns),
            transcendentals=0,
        ),
    )(place, *amplitudes, *[piece for quarter in quarters for piece in quarter])


def place_kernel(count, at_ref, *refs):
    blocks, out_ref = refs[:count], refs[-1]
    width = sum(ref.shape[2] for ref in blocks)
    for s in range(GROUP):
        start = s * width
        for ref in blocks:
            out_ref[:, start : start + ref.shape[2]] = ref[s]
            start += ref.shape[2]


def place(at, blocks, out=None):
    sources, rows, _ = blocks[0].shape
    width = sum(block.shape[2] for block in blocks)
    steps = sources // GROUP
    count = len(blocks)
    return pl.pallas_call(
        functools.partial(place_kernel, count),
        grid_spec=pltpu.PrefetchScalarGridSpec(
            num_scalar_prefetch=1,
            grid=(steps,),
            in_specs=[
                pl.BlockSpec((GROUP, rows, block.shape[2]), lambda g, at: (g, 0, 0))
                for block in blocks
            ]
            + ([] if out is None else [pl.BlockSpec(memory_space=pl.ANY)]),
            out_specs=pl.BlockSpec((rows, GROUP * width), lambda g, at: (0, at[0] * steps + g)),
        ),
        out_shape=jax.ShapeDtypeStruct((rows, 2 * sources * width), jnp.float32),
        input_output_aliases={} if out is None else {1 + count: 0},
        compiler_params=pltpu.CompilerParams(vmem_limit_bytes=16 << 20),
        cost_estimate=pl.CostEstimate(
            flops=0, bytes_accessed=8 * sources * rows * width, transcendentals=0
        ),
    )(at, *blocks, *([] if out is None else [out]))


def gather_amplitudes(amplitudes):
    rows, depth = amplitudes.shape
    part = depth // 4
    last = amplitudes[:, 3 * part :]
    last = jnp.concatenate([last] + [shift_x(last, -d) for d in (1, 2, 3)])
    last = lax.all_gather(last, "z", axis=0).reshape(8, 4, rows, part)
    here = jnp.broadcast_to(amplitudes[None, :, : 3 * part], (8, rows, 3 * part))
    here = lax.all_to_all(here, "z", split_axis=0, concat_axis=0, tiled=True).reshape(-1, 3 * part)
    ahead, behind = shift_x(here, -1), shift_x(here, 1)
    half = here.shape[0] // 2
    low, high = shift_x(ahead[:half], -1), shift_x(behind[half:], 1)
    return [here, ahead, behind, low, high, last]


def on_device(amplitudes, integrals):
    x, yl, yh, core = (lax.axis_index(name) for name in ("x", "yl", "yh", "core"))
    rows = amplitudes.shape[0]
    columns = integrals.shape[1]
    spot = jnp.stack([2 * yh + core, x])
    t = gather_amplitudes(amplitudes)

    own = [integrals.T[:CUT], integrals.T[CUT:]]
    near, far = [swap_near(v) for v in own], [swap_far(v) for v in own]
    across = [swap_far(near[0]), swap_near(far[1])]

    def exchange(v):
        return lax.all_to_all(
            v.reshape(-1, rows, v.shape[1]), ("x", "z"), split_axis=0, concat_axis=0, tiled=True
        )

    other_block = [
        exchange(product(spot, t, [[n], [swap_core(n)], [f], [swap_core(f)]]))
        for n, f in zip(near, far)
    ]
    own2, across2 = [swap_core(v) for v in own], [swap_core(v) for v in across]
    own_block = exchange(product(spot, t, [own, own2, across, across2]))
    out = place((1 - yl).reshape(1), other_block)
    return place(yl.reshape(1), [own_block], out)


def solution(mesh):
    grid = Mesh(mesh.devices.reshape(2, 4, 8, 2, 2), AXES)
    return jax.shard_map(
        on_device,
        mesh=grid,
        in_specs=(P(AXES, None), P(("yh", "core"), ("yl", "x", "z"))),
        out_specs=P(AXES, None),
        check_vma=False,
    )
```

```python
import functools
import math

import jax
import jax.numpy as jnp
from jax import lax
from jax.experimental import pallas as pl
from jax.experimental.pallas import tpu as pltpu
from jax.sharding import Mesh, PartitionSpec as P

AXES = ("yl", "x", "z", "yh", "core")
TILE = 256
CUT = 768
ORDER = (1, 7, 3, 5, 2, 6, 4)
GROUP = 16


def swap_core(value):
    return lax.ppermute(value, "core", [(0, 1), (1, 0)])


def shift_x(value, by):
    return lax.ppermute(value, "x", [(i, (i + by) % 4) for i in range(4)])


def shift_z(value, by):
    return lax.ppermute(value, "z", [(i, (i + by) % 8) for i in range(8)])


def swap_near(value):
    return lax.ppermute(value, "yl", [(0, 1), (1, 0)])


def swap_far(value):
    return lax.ppermute(value, ("yl", "yh"), [(2, 1), (1, 2), (3, 0), (0, 3)])


def halves(value):
    top = value.astype(jnp.bfloat16)
    rest = (value - top.astype(jnp.float32)).astype(jnp.bfloat16)
    return top, rest


def load_amplitudes(place_ref, around, first_refs, last_ref, top_ref, rest_ref):
    here_ref, ahead_ref, low_ref, high_ref, behind_ref = first_refs
    own, x, z = place_ref[0], place_ref[1], place_ref[2]
    heights, _, rows, half = last_ref.shape
    part = half // 2

    @pl.loop(0, 4 * heights)
    def _(i):
        q, there = i // heights, lax.rem(i, heights)
        source = own ^ q
        take = pl.ds(pl.multiple_of((source & 1) * part, part), part)
        into = pl.ds(pl.multiple_of(q * part, part), part)
        below = there < heights // 2
        opposite = jnp.where(
            below,
            low_ref[jnp.minimum(there, heights // 2 - 1), :, take],
            high_ref[jnp.maximum(there - heights // 2, 0), :, take],
        )
        first = [here_ref[there, :, take], ahead_ref[there, :, take], opposite, behind_ref[there, :, take]]
        for d in range(4):
            value = jnp.where(source < 2, first[d], last_ref[there, d, :, take])
            if around:
                row = lax.rem(there - z + heights, heights) * (4 * rows) + d * rows
            else:
                row = lax.rem(x + d, 4) * (heights * rows) + there * rows
            into_rows = pl.ds(pl.multiple_of(row, rows), rows)
            top_ref[into_rows, into], rest_ref[into_rows, into] = halves(value)


def product_kernel(around, counts, place_ref, *refs):
    pieces = refs[6 : 6 + sum(len(tiles) for tiles in counts)]
    outs, (top_ref, rest_ref) = refs[6 + len(pieces) : -2], refs[-2:]

    @pl.when(pl.program_id(0) == 0)
    def _():
        load_amplitudes(place_ref, around, refs[:5], refs[5], top_ref, rest_ref)

    dot = functools.partial(
        lax.dot_general,
        dimension_numbers=(((1,), (1,)), ((), ())),
        preferred_element_type=jnp.float32,
    )
    total, at = None, 0
    for q, tiles in enumerate(counts):
        value, start = pieces[at][...], tiles[0]
        for i, count in enumerate(tiles[1:]):
            value = jnp.where(pl.program_id(0) < start, value, pieces[at + 1 + i][...])
            start += count
        at += len(tiles)
        top, rest = halves(value)
        depth = pl.ds(q * value.shape[1], value.shape[1])
        t_top, t_rest = top_ref[:, depth], rest_ref[:, depth]
        term = dot(t_top, rest) + dot(t_rest, top) + dot(t_top, top)
        total = term if total is None else total + term
    count = total.shape[0] // len(outs)
    for i, out_ref in enumerate(outs):
        out_ref[...] = 0.5 * total[i * count : (i + 1) * count]


def product(place, amplitudes, quarters, around=False):
    last = amplitudes[-1]
    rows, depth = math.prod(last.shape[:3]), 2 * last.shape[3]
    part = depth // 4
    outs = last.shape[0] if around else 1
    columns = sum(piece.shape[0] for piece in quarters[0])
    specs, counts = [], []
    for quarter in quarters:
        start, tiles = 0, []
        for piece in quarter:
            count = pl.cdiv(piece.shape[0], TILE)
            specs.append(
                pl.BlockSpec(
                    (TILE, part),
                    lambda n, place, start=start, count=count: (jnp.clip(n - start, 0, count - 1), 0),
                )
            )
            tiles.append(count)
            start += count
        counts.append(tiles)
    whole = [
        pl.BlockSpec(v.shape, lambda n, place, v=v: (0,) * v.ndim, pipeline_mode=pl.Buffered(1))
        for v in amplitudes
    ]
    return pl.pallas_call(
        functools.partial(product_kernel, around, counts),
        grid_spec=pltpu.PrefetchScalarGridSpec(
            num_scalar_prefetch=1,
            grid=(pl.cdiv(columns, TILE),),
            in_specs=whole + specs,
            out_specs=[pl.BlockSpec((rows // outs, TILE), lambda n, place: (0, n))] * outs,
            scratch_shapes=[pltpu.VMEM((rows, depth), jnp.bfloat16)] * 2,
        ),
        out_shape=[jax.ShapeDtypeStruct((rows // outs, columns), jnp.float32)] * outs,
        compiler_params=pltpu.CompilerParams(vmem_limit_bytes=60 << 20),
        cost_estimate=pl.CostEstimate(
            flops=6 * rows * depth * columns,
            bytes_accessed=4 * (rows * depth + depth * columns + rows * columns),
            transcendentals=0,
        ),
    )(place, *amplitudes, *[piece for quarter in quarters for piece in quarter])


def regroup_kernel(chunks, z_ref, *refs):
    heights = len(refs[: -4]) // chunks
    outs = refs[-4:]
    for e in range(heights):
        source = lax.rem(z_ref[0] - e + heights, heights)
        at = 0
        for c in range(chunks):
            piece_ref = refs[c * heights + e]
            width = piece_ref.shape[2]
            for d, out_ref in enumerate(outs):
                out_ref[source, :, at : at + width] = piece_ref[d]
            at += width


def regroup(z, chunks):
    heights = len(chunks[0])
    _, rows, _ = chunks[0][0].shape
    width = sum(chunk[0].shape[2] for chunk in chunks)
    pieces = [piece for chunk in chunks for piece in chunk]
    return pl.pallas_call(
        functools.partial(regroup_kernel, len(chunks)),
        grid_spec=pltpu.PrefetchScalarGridSpec(
            num_scalar_prefetch=1,
            grid=(1,),
            in_specs=[pl.BlockSpec(v.shape, lambda n, z: (0, 0, 0)) for v in pieces],
            out_specs=[pl.BlockSpec((heights, rows, width), lambda n, z: (0, 0, 0))] * 4,
        ),
        out_shape=[jax.ShapeDtypeStruct((heights, rows, width), jnp.float32)] * 4,
        compiler_params=pltpu.CompilerParams(vmem_limit_bytes=32 << 20),
        cost_estimate=pl.CostEstimate(
            flops=0, bytes_accessed=32 * heights * rows * width, transcendentals=0
        ),
    )(z, *pieces)


def place_kernel(at_ref, block_ref, _, out_ref):
    width = block_ref.shape[2]
    for s in range(GROUP):
        out_ref[:, s * width : (s + 1) * width] = block_ref[s]


def place(at, block, out):
    sources, rows, width = block.shape
    steps = sources // GROUP
    return pl.pallas_call(
        place_kernel,
        grid_spec=pltpu.PrefetchScalarGridSpec(
            num_scalar_prefetch=1,
            grid=(steps,),
            in_specs=[
                pl.BlockSpec((GROUP, rows, width), lambda g, at: (g, 0, 0)),
                pl.BlockSpec(memory_space=pl.ANY),
            ],
            out_specs=pl.BlockSpec((rows, GROUP * width), lambda g, at: (0, at[0] * steps + g)),
        ),
        out_shape=jax.ShapeDtypeStruct(out.shape, jnp.float32),
        input_output_aliases={2: 0},
        compiler_params=pltpu.CompilerParams(vmem_limit_bytes=16 << 20),
        cost_estimate=pl.CostEstimate(
            flops=0, bytes_accessed=8 * sources * rows * width, transcendentals=0
        ),
    )(at, block, out)


def place_by_x_kernel(at_ref, *refs):
    blocks, out_ref, by_source_ref = refs[:-2], refs[-2], refs[-1]
    heights, _, width = blocks[0].shape

    @pl.when(pl.program_id(0) == 0)
    def _():
        for d, ref in enumerate(blocks):
            source = lax.rem(at_ref[1] - d + 4, 4) * heights

            @pl.loop(0, heights)
            def _(s, ref=ref, source=source):
                by_source_ref[source + s] = ref[s]

    for s in range(GROUP):
        out_ref[:, s * width : (s + 1) * width] = by_source_ref[pl.program_id(0) * GROUP + s]


def place_by_x(at, blocks):
    heights, rows, width = blocks[0].shape
    steps = 4 * heights // GROUP
    return pl.pallas_call(
        place_by_x_kernel,
        grid_spec=pltpu.PrefetchScalarGridSpec(
            num_scalar_prefetch=1,
            grid=(steps,),
            in_specs=[pl.BlockSpec((heights, rows, width), lambda g, at: (0, 0, 0))] * 4,
            out_specs=pl.BlockSpec((rows, GROUP * width), lambda g, at: (0, at[0] * steps + g)),
            scratch_shapes=[pltpu.VMEM((4 * heights, rows, width), jnp.float32)],
        ),
        out_shape=jax.ShapeDtypeStruct((rows, 8 * heights * width), jnp.float32),
        compiler_params=pltpu.CompilerParams(vmem_limit_bytes=32 << 20),
        cost_estimate=pl.CostEstimate(
            flops=0, bytes_accessed=32 * heights * rows * width, transcendentals=0
        ),
    )(at, *blocks)


def after(value, *others):
    return lax.optimization_barrier((value, *others))[0]


def on_device(amplitudes, integrals):
    x, z, yl, yh, core = (lax.axis_index(name) for name in ("x", "z", "yl", "yh", "core"))
    rows, depth = amplitudes.shape
    columns = integrals.shape[1]
    half = depth // 2
    spot = jnp.stack([2 * yh + core, x, z])

    turns = [shift_x(amplitudes[:, half:], -d) for d in (1, 2, 3)]
    last = jnp.concatenate([amplitudes[:, half:]] + turns)
    here = jnp.broadcast_to(after(amplitudes[:, :half], turns[2])[None], (8, rows, half))
    here = lax.all_to_all(here, "z", split_axis=0, concat_axis=0, tiled=True)
    here = after(here, last)
    last = lax.all_gather(last, "z", axis=0).reshape(8, 4, rows, half)
    ahead, behind = shift_x(here, -1), shift_x(here, 1)
    low, high = shift_x(ahead[:4], -1), shift_x(behind[4:], 1)
    t = (here, ahead, low, high, behind, last)

    own = after(integrals.T, *turns)
    near, far = swap_near(own), swap_far(own)
    near, far = after((near, far), low, high)
    across = [swap_far(near[:CUT]), swap_near(far[CUT:])]
    results = product(spot, t, [[near], [swap_core(near)], [far], [swap_core(far)]], around=True)
    sent = {e: shift_z(results[e], e) for e in ORDER}
    own2 = swap_core(after(own, here))
    across = after(across, sent[3], sent[5])
    across2 = [swap_core(v) for v in across]
    t = after(t, sent[3], sent[5])
    (own_block,) = product(spot, t, [[own], [own2], across, across2])
    own_block = after(own_block, *sent.values())
    own_block = lax.all_to_all(
        own_block.reshape(32, rows, columns), ("x", "z"), split_axis=0, concat_axis=0, tiled=True
    )
    chunks = [[v.reshape(4, rows, columns) for v in [results[0]] + [sent[e] for e in range(1, 8)]]]
    by_x = regroup(z.reshape(1), chunks)
    by_x = [by_x[0]] + [shift_x(by_x[d], d) for d in (1, 2, 3)]
    out = place_by_x(jnp.stack([1 - yl, x]), by_x)
    return place(yl.reshape(1), own_block, out)


def solution(mesh):
    grid = Mesh(mesh.devices.reshape(2, 4, 8, 2, 2), AXES)
    return jax.shard_map(
        on_device,
        mesh=grid,
        in_specs=(P(AXES, None), P(("yh", "core"), ("yl", "x", "z"))),
        out_specs=P(AXES, None),
        check_vma=False,
    )
```

```python
import functools
import math

import jax
import jax.numpy as jnp
from jax import lax
from jax.experimental import pallas as pl
from jax.experimental.pallas import tpu as pltpu
from jax.sharding import Mesh, PartitionSpec as P

AXES = ("yl", "x", "z", "yh", "core")
TILE = 256
CUT = 1024
GROUP = 16


def swap_core(value):
    return lax.ppermute(value, "core", [(0, 1), (1, 0)])


def shift_x(value, by):
    return lax.ppermute(value, "x", [(i, (i + by) % 4) for i in range(4)])


def swap_near(value):
    return lax.ppermute(value, "yl", [(0, 1), (1, 0)])


def swap_far(value):
    return lax.ppermute(value, ("yl", "yh"), [(2, 1), (1, 2), (3, 0), (0, 3)])


def halves(value):
    top = value.astype(jnp.bfloat16)
    rest = (value - top.astype(jnp.float32)).astype(jnp.bfloat16)
    return top, rest


def load_amplitudes(place_ref, around, first_refs, last_ref, top_ref, rest_ref):
    here_ref, ahead_ref, low_ref, high_ref, behind_ref = first_refs
    own, x, z = place_ref[0], place_ref[1], place_ref[2]
    heights, _, rows, half = last_ref.shape
    part = half // 2

    @pl.loop(0, 4 * heights)
    def _(i):
        q, there = i // heights, lax.rem(i, heights)
        source = own ^ q
        take = pl.ds(pl.multiple_of((source & 1) * part, part), part)
        into = pl.ds(pl.multiple_of(q * part, part), part)
        below = there < heights // 2
        opposite = jnp.where(
            below,
            low_ref[jnp.minimum(there, heights // 2 - 1), :, take],
            high_ref[jnp.maximum(there - heights // 2, 0), :, take],
        )
        first = [here_ref[there, :, take], ahead_ref[there, :, take], opposite, behind_ref[there, :, take]]
        for d in range(4):
            value = jnp.where(source < 2, first[d], last_ref[there, d, :, take])
            if around:
                row = lax.rem(there - z + heights, heights) * (4 * rows) + d * rows
            else:
                row = lax.rem(x + d, 4) * (heights * rows) + there * rows
            into_rows = pl.ds(pl.multiple_of(row, rows), rows)
            top_ref[into_rows, into], rest_ref[into_rows, into] = halves(value)


def product_kernel(around, counts, place_ref, *refs):
    pieces = refs[6 : 6 + sum(len(tiles) for tiles in counts)]
    outs, (top_ref, rest_ref) = refs[6 + len(pieces) : -2], refs[-2:]

    @pl.when(pl.program_id(0) == 0)
    def _():
        load_amplitudes(place_ref, around, refs[:5], refs[5], top_ref, rest_ref)

    dot = functools.partial(
        lax.dot_general,
        dimension_numbers=(((1,), (1,)), ((), ())),
        preferred_element_type=jnp.float32,
    )
    total, at = None, 0
    for q, tiles in enumerate(counts):
        value, start = pieces[at][...], tiles[0]
        for i, count in enumerate(tiles[1:]):
            value = jnp.where(pl.program_id(0) < start, value, pieces[at + 1 + i][...])
            start += count
        at += len(tiles)
        top, rest = halves(value)
        depth = pl.ds(q * value.shape[1], value.shape[1])
        t_top, t_rest = top_ref[:, depth], rest_ref[:, depth]
        term = dot(t_top, rest) + dot(t_rest, top) + dot(t_top, top)
        total = term if total is None else total + term
    count = total.shape[0] // len(outs)
    for i, out_ref in enumerate(outs):
        out_ref[...] = 0.5 * total[i * count : (i + 1) * count]


def product(place, amplitudes, quarters, around=False):
    last = amplitudes[-1]
    rows, depth = math.prod(last.shape[:3]), 2 * last.shape[3]
    part = depth // 4
    outs = last.shape[0] if around else 1
    columns = sum(piece.shape[0] for piece in quarters[0])
    specs, counts = [], []
    for quarter in quarters:
        start, tiles = 0, []
        for piece in quarter:
            count = pl.cdiv(piece.shape[0], TILE)
            specs.append(
                pl.BlockSpec(
                    (TILE, part),
                    lambda n, place, start=start, count=count: (jnp.clip(n - start, 0, count - 1), 0),
                )
            )
            tiles.append(count)
            start += count
        counts.append(tiles)
    whole = [
        pl.BlockSpec(v.shape, lambda n, place, v=v: (0,) * v.ndim, pipeline_mode=pl.Buffered(1))
        for v in amplitudes
    ]
    return pl.pallas_call(
        functools.partial(product_kernel, around, counts),
        grid_spec=pltpu.PrefetchScalarGridSpec(
            num_scalar_prefetch=1,
            grid=(pl.cdiv(columns, TILE),),
            in_specs=whole + specs,
            out_specs=[pl.BlockSpec((rows // outs, TILE), lambda n, place: (0, n))] * outs,
            scratch_shapes=[pltpu.VMEM((rows, depth), jnp.bfloat16)] * 2,
        ),
        out_shape=[jax.ShapeDtypeStruct((rows // outs, columns), jnp.float32)] * outs,
        compiler_params=pltpu.CompilerParams(vmem_limit_bytes=60 << 20),
        cost_estimate=pl.CostEstimate(
            flops=6 * rows * depth * columns,
            bytes_accessed=4 * (rows * depth + depth * columns + rows * columns),
            transcendentals=0,
        ),
    )(place, *amplitudes, *[piece for quarter in quarters for piece in quarter])


def place_kernel(count, at_ref, *refs):
    blocks, out_ref = refs[:count], refs[-1]
    width = sum(ref.shape[2] for ref in blocks)
    for s in range(GROUP):
        start = s * width
        for ref in blocks:
            out_ref[:, start : start + ref.shape[2]] = ref[s]
            start += ref.shape[2]


def place(at, blocks, out=None):
    sources, rows, _ = blocks[0].shape
    width = sum(block.shape[2] for block in blocks)
    steps = sources // GROUP
    count = len(blocks)
    return pl.pallas_call(
        functools.partial(place_kernel, count),
        grid_spec=pltpu.PrefetchScalarGridSpec(
            num_scalar_prefetch=1,
            grid=(steps,),
            in_specs=[
                pl.BlockSpec((GROUP, rows, block.shape[2]), lambda g, at: (g, 0, 0))
                for block in blocks
            ]
            + ([] if out is None else [pl.BlockSpec(memory_space=pl.ANY)]),
            out_specs=pl.BlockSpec((rows, GROUP * width), lambda g, at: (0, at[0] * steps + g)),
        ),
        out_shape=jax.ShapeDtypeStruct((rows, 2 * sources * width), jnp.float32),
        input_output_aliases={} if out is None else {1 + count: 0},
        compiler_params=pltpu.CompilerParams(vmem_limit_bytes=16 << 20),
        cost_estimate=pl.CostEstimate(
            flops=0, bytes_accessed=8 * sources * rows * width, transcendentals=0
        ),
    )(at, *blocks, *([] if out is None else [out]))


def after(value, *others):
    return lax.optimization_barrier((value, *others))[0]


def on_device(amplitudes, integrals):
    x, z, yl, yh, core = (lax.axis_index(name) for name in ("x", "z", "yl", "yh", "core"))
    rows, depth = amplitudes.shape
    columns = integrals.shape[1]
    half = depth // 2
    spot = jnp.stack([2 * yh + core, x, z])

    turns = [shift_x(amplitudes[:, half:], -d) for d in (1, 2, 3)]
    last = jnp.concatenate([amplitudes[:, half:]] + turns)
    here = jnp.broadcast_to(after(amplitudes[:, :half], last)[None], (8, rows, half))
    here = lax.all_to_all(here, "z", split_axis=0, concat_axis=0, tiled=True)
    last = lax.all_gather(last, "z", axis=0).reshape(8, 4, rows, half)
    ahead, behind = shift_x(here, -1), shift_x(here, 1)
    low, high = shift_x(ahead[:4], -1), shift_x(behind[4:], 1)
    t = (here, ahead, low, high, behind, last)

    first, second = after(integrals.T[:CUT], *turns), after(integrals.T[CUT:], ahead, behind)
    near, far = after((swap_near(first), swap_far(first)), low, high)
    near_next, far_next = swap_near(second), swap_far(second)

    def exchange(v):
        return lax.all_to_all(
            v.reshape(-1, rows, v.shape[1]), ("x", "z"), split_axis=0, concat_axis=0, tiled=True
        )

    (result,) = product(spot, t, [[near], [swap_core(near)], [far], [swap_core(far)]])
    t = after(t, result)
    near_next, far_next = after((near_next, far_next), result)
    across = [swap_far(after(near, low, high)), swap_near(far_next)]
    own = [first, second]
    own2 = [swap_core(v) for v in after((first, second), result)]
    (result_next,) = product(
        spot, t, [[near_next], [swap_core(near_next)], [far_next], [swap_core(far_next)]]
    )
    t = after(t, result_next)
    other_block = [exchange(result)]
    other_block.append(exchange(after(result_next, other_block[0])))
    across2 = [swap_core(v) for v in after(across, result_next)]
    (own_block,) = product(spot, t, [own, own2, across, across2])
    own_block = exchange(after(own_block, other_block[1]))
    out = place((1 - yl).reshape(1), other_block)
    return place(yl.reshape(1), [own_block], out)


def solution(mesh):
    grid = Mesh(mesh.devices.reshape(2, 4, 8, 2, 2), AXES)
    return jax.shard_map(
        on_device,
        mesh=grid,
        in_specs=(P(AXES, None), P(("yh", "core"), ("yl", "x", "z"))),
        out_specs=P(AXES, None),
        check_vma=False,
    )
```

```python
import functools
import math

import jax
import jax.numpy as jnp
from jax import lax
from jax.experimental import pallas as pl
from jax.experimental.pallas import tpu as pltpu
from jax.sharding import Mesh, PartitionSpec as P

AXES = ("yl", "x", "z", "yh", "core")
TILE = 256
CUT = 768
GROUP = 16


def swap_core(value):
    return lax.ppermute(value, "core", [(0, 1), (1, 0)])


def shift_x(value, by):
    return lax.ppermute(value, "x", [(i, (i + by) % 4) for i in range(4)])


def swap_near(value):
    return lax.ppermute(value, "yl", [(0, 1), (1, 0)])


def swap_far(value):
    return lax.ppermute(value, ("yl", "yh"), [(2, 1), (1, 2), (3, 0), (0, 3)])


def halves(value):
    top = value.astype(jnp.bfloat16)
    rest = (value - top.astype(jnp.float32)).astype(jnp.bfloat16)
    return top, rest


def load_amplitudes(place_ref, around, first_refs, last_ref, top_ref, rest_ref):
    here_ref, ahead_ref, low_ref, high_ref, behind_ref = first_refs
    own, x, z = place_ref[0], place_ref[1], place_ref[2]
    heights, _, rows, half = last_ref.shape
    part = half // 2

    @pl.loop(0, 4 * heights)
    def _(i):
        q, there = i // heights, lax.rem(i, heights)
        source = own ^ q
        take = pl.ds(pl.multiple_of((source & 1) * part, part), part)
        into = pl.ds(pl.multiple_of(q * part, part), part)
        below = there < heights // 2
        opposite = jnp.where(
            below,
            low_ref[jnp.minimum(there, heights // 2 - 1), :, take],
            high_ref[jnp.maximum(there - heights // 2, 0), :, take],
        )
        first = [here_ref[there, :, take], ahead_ref[there, :, take], opposite, behind_ref[there, :, take]]
        for d in range(4):
            value = jnp.where(source < 2, first[d], last_ref[there, d, :, take])
            if around:
                row = lax.rem(there - z + heights, heights) * (4 * rows) + d * rows
            else:
                row = lax.rem(x + d, 4) * (heights * rows) + there * rows
            into_rows = pl.ds(pl.multiple_of(row, rows), rows)
            top_ref[into_rows, into], rest_ref[into_rows, into] = halves(value)


def product_kernel(around, counts, place_ref, *refs):
    pieces = refs[6 : 6 + sum(len(tiles) for tiles in counts)]
    outs, (top_ref, rest_ref) = refs[6 + len(pieces) : -2], refs[-2:]

    @pl.when(pl.program_id(0) == 0)
    def _():
        load_amplitudes(place_ref, around, refs[:5], refs[5], top_ref, rest_ref)

    dot = functools.partial(
        lax.dot_general,
        dimension_numbers=(((1,), (1,)), ((), ())),
        preferred_element_type=jnp.float32,
    )
    total, at = None, 0
    for q, tiles in enumerate(counts):
        value, start = pieces[at][...], tiles[0]
        for i, count in enumerate(tiles[1:]):
            value = jnp.where(pl.program_id(0) < start, value, pieces[at + 1 + i][...])
            start += count
        at += len(tiles)
        top, rest = halves(value)
        depth = pl.ds(q * value.shape[1], value.shape[1])
        t_top, t_rest = top_ref[:, depth], rest_ref[:, depth]
        term = dot(t_top, rest) + dot(t_rest, top) + dot(t_top, top)
        total = term if total is None else total + term
    count = total.shape[0] // len(outs)
    for i, out_ref in enumerate(outs):
        out_ref[...] = 0.5 * total[i * count : (i + 1) * count]


def product(place, amplitudes, quarters, around=False):
    last = amplitudes[-1]
    rows, depth = math.prod(last.shape[:3]), 2 * last.shape[3]
    part = depth // 4
    outs = last.shape[0] if around else 1
    columns = sum(piece.shape[0] for piece in quarters[0])
    specs, counts = [], []
    for quarter in quarters:
        start, tiles = 0, []
        for piece in quarter:
            count = pl.cdiv(piece.shape[0], TILE)
            specs.append(
                pl.BlockSpec(
                    (TILE, part),
                    lambda n, place, start=start, count=count: (jnp.clip(n - start, 0, count - 1), 0),
                )
            )
            tiles.append(count)
            start += count
        counts.append(tiles)
    whole = [
        pl.BlockSpec(v.shape, lambda n, place, v=v: (0,) * v.ndim, pipeline_mode=pl.Buffered(1))
        for v in amplitudes
    ]
    return pl.pallas_call(
        functools.partial(product_kernel, around, counts),
        grid_spec=pltpu.PrefetchScalarGridSpec(
            num_scalar_prefetch=1,
            grid=(pl.cdiv(columns, TILE),),
            in_specs=whole + specs,
            out_specs=[pl.BlockSpec((rows // outs, TILE), lambda n, place: (0, n))] * outs,
            scratch_shapes=[pltpu.VMEM((rows, depth), jnp.bfloat16)] * 2,
        ),
        out_shape=[jax.ShapeDtypeStruct((rows // outs, columns), jnp.float32)] * outs,
        compiler_params=pltpu.CompilerParams(vmem_limit_bytes=60 << 20),
        cost_estimate=pl.CostEstimate(
            flops=6 * rows * depth * columns,
            bytes_accessed=4 * (rows * depth + depth * columns + rows * columns),
            transcendentals=0,
        ),
    )(place, *amplitudes, *[piece for quarter in quarters for piece in quarter])


def place_kernel(count, at_ref, *refs):
    blocks, out_ref = refs[:count], refs[-1]
    width = sum(ref.shape[2] for ref in blocks)
    for s in range(GROUP):
        start = s * width
        for ref in blocks:
            out_ref[:, start : start + ref.shape[2]] = ref[s]
            start += ref.shape[2]


def place(at, blocks, out=None):
    sources, rows, _ = blocks[0].shape
    width = sum(block.shape[2] for block in blocks)
    steps = sources // GROUP
    count = len(blocks)
    return pl.pallas_call(
        functools.partial(place_kernel, count),
        grid_spec=pltpu.PrefetchScalarGridSpec(
            num_scalar_prefetch=1,
            grid=(steps,),
            in_specs=[
                pl.BlockSpec((GROUP, rows, block.shape[2]), lambda g, at: (g, 0, 0))
                for block in blocks
            ]
            + ([] if out is None else [pl.BlockSpec(memory_space=pl.ANY)]),
            out_specs=pl.BlockSpec((rows, GROUP * width), lambda g, at: (0, at[0] * steps + g)),
        ),
        out_shape=jax.ShapeDtypeStruct((rows, 2 * sources * width), jnp.float32),
        input_output_aliases={} if out is None else {1 + count: 0},
        compiler_params=pltpu.CompilerParams(vmem_limit_bytes=16 << 20),
        cost_estimate=pl.CostEstimate(
            flops=0, bytes_accessed=8 * sources * rows * width, transcendentals=0
        ),
    )(at, *blocks, *([] if out is None else [out]))


def after(value, *others):
    return lax.optimization_barrier((value, *others))[0]


def on_device(amplitudes, integrals):
    x, z, yl, yh, core = (lax.axis_index(name) for name in ("x", "z", "yl", "yh", "core"))
    rows, depth = amplitudes.shape
    columns = integrals.shape[1]
    half = depth // 2
    spot = jnp.stack([2 * yh + core, x, z])

    turns = [shift_x(amplitudes[:, half:], -d) for d in (1, 2, 3)]
    last = jnp.concatenate([amplitudes[:, half:]] + turns)
    here = jnp.broadcast_to(after(amplitudes[:, :half], last)[None], (8, rows, half))
    here = lax.all_to_all(here, "z", split_axis=0, concat_axis=0, tiled=True)
    last = lax.all_gather(last, "z", axis=0).reshape(8, 4, rows, half)
    ahead, behind = shift_x(here, -1), shift_x(here, 1)
    low, high = shift_x(ahead[:4], -1), shift_x(behind[4:], 1)
    t = (here, ahead, low, high, behind, last)

    first, second = after(integrals.T[:CUT], low, high), integrals.T[CUT:]
    near, far = after((swap_near(first), swap_far(first)), ahead, behind)
    near_next, far_next = after((swap_near(second), swap_far(second)), ahead, behind)

    def exchange(v):
        return lax.all_to_all(
            v.reshape(-1, rows, v.shape[1]), ("x", "z"), split_axis=0, concat_axis=0, tiled=True
        )

    (result,) = product(spot, t, [[near], [swap_core(near)], [far], [swap_core(far)]])
    (result_next,) = product(
        spot, t, [[near_next], [swap_core(near_next)], [far_next], [swap_core(far_next)]]
    )
    other_block = [exchange(result), exchange(result_next)]
    across = [swap_far(near), swap_near(far_next)]
    own, own2, across2 = [first, second], [swap_core(first), swap_core(second)], [swap_core(v) for v in across]
    (own_block,) = product(spot, t, [own, own2, across, across2])
    own_block = exchange(after(own_block, other_block[1]))
    out = place((1 - yl).reshape(1), other_block)
    return place(yl.reshape(1), [own_block], out)


def solution(mesh):
    grid = Mesh(mesh.devices.reshape(2, 4, 8, 2, 2), AXES)
    return jax.shard_map(
        on_device,
        mesh=grid,
        in_specs=(P(AXES, None), P(("yh", "core"), ("yl", "x", "z"))),
        out_specs=P(AXES, None),
        check_vma=False,
    )
```

```python
import functools
import math

import jax
import jax.numpy as jnp
from jax import lax
from jax.experimental import pallas as pl
from jax.experimental.pallas import tpu as pltpu
from jax.sharding import Mesh, PartitionSpec as P

AXES = ("yl", "x", "z", "yh", "core")
TILE = 256
CUT = 3
GROUP = 16


def swap_core(value):
    return lax.ppermute(value, "core", [(0, 1), (1, 0)])


def shift_x(value, by):
    return lax.ppermute(value, "x", [(i, (i + by) % 4) for i in range(4)])


def swap_near(value):
    return lax.ppermute(value, "yl", [(0, 1), (1, 0)])


def swap_far(value):
    return lax.ppermute(value, ("yl", "yh"), [(2, 1), (1, 2), (3, 0), (0, 3)])


def halves(value):
    top = value.astype(jnp.bfloat16)
    rest = (value - top.astype(jnp.float32)).astype(jnp.bfloat16)
    return top, rest


def load_amplitudes(place_ref, first_refs, last_ref, top_ref, rest_ref):
    here_ref, ahead_ref, low_ref, high_ref, behind_ref = first_refs
    own, x = place_ref[0], place_ref[1]
    heights, _, rows, half = last_ref.shape
    part = half // 2

    @pl.loop(0, 4 * heights)
    def _(i):
        q, there = i // heights, lax.rem(i, heights)
        source = own ^ q
        take = pl.ds(pl.multiple_of((source & 1) * part, part), part)
        into = pl.ds(pl.multiple_of(q * part, part), part)
        below = there < heights // 2
        opposite = jnp.where(
            below,
            low_ref[jnp.minimum(there, heights // 2 - 1), :, take],
            high_ref[jnp.maximum(there - heights // 2, 0), :, take],
        )
        first = [here_ref[there, :, take], ahead_ref[there, :, take], opposite, behind_ref[there, :, take]]
        for d in range(4):
            value = jnp.where(source < 2, first[d], last_ref[there, d, :, take])
            row = lax.rem(x + d, 4) * (heights * rows) + there * rows
            into_rows = pl.ds(pl.multiple_of(row, rows), rows)
            top_ref[into_rows, into], rest_ref[into_rows, into] = halves(value)


def product_kernel(counts, lo, place_ref, *refs):
    pieces = refs[6 : 6 + sum(len(tiles) for tiles in counts)]
    out_ref, top_ref, rest_ref = refs[-3:]

    @pl.when(pl.program_id(0) == 0)
    def _():
        load_amplitudes(place_ref, refs[:5], refs[5], top_ref, rest_ref)

    dot = functools.partial(
        lax.dot_general,
        dimension_numbers=(((1,), (1,)), ((), ())),
        preferred_element_type=jnp.float32,
    )
    total, at = None, 0
    for q, tiles in enumerate(counts):
        value, start = pieces[at][...], tiles[0] - lo
        for i, count in enumerate(tiles[1:]):
            value = jnp.where(pl.program_id(0) < start, value, pieces[at + 1 + i][...])
            start += count
        at += len(tiles)
        top, rest = halves(value)
        depth = pl.ds(q * value.shape[1], value.shape[1])
        t_top, t_rest = top_ref[:, depth], rest_ref[:, depth]
        term = dot(t_top, rest) + dot(t_rest, top) + dot(t_top, top)
        total = term if total is None else total + term
    out_ref[...] = 0.5 * total


def product(place, amplitudes, quarters, tiles=None, columns=None, out=None):
    last = amplitudes[-1]
    rows, depth = math.prod(last.shape[:3]), 2 * last.shape[3]
    part = depth // 4
    whole_count = sum(piece.shape[0] for piece in quarters[0])
    lo, hi = tiles or (0, pl.cdiv(whole_count, TILE))
    count = min(hi * TILE, whole_count) - lo * TILE
    columns = out.shape[1] if out is not None else columns or count
    skip = (columns - count) // TILE if out is not None else 0
    specs, counts = [], []
    for quarter in quarters:
        start, sizes = -lo, []
        for piece in quarter:
            size = pl.cdiv(piece.shape[0], TILE)
            specs.append(
                pl.BlockSpec(
                    (TILE, part),
                    lambda n, place, start=start, size=size: (jnp.clip(n - start, 0, size - 1), 0),
                )
            )
            sizes.append(size)
            start += size
        counts.append(sizes)
    whole = [
        pl.BlockSpec(v.shape, lambda n, place, v=v: (0,) * v.ndim, pipeline_mode=pl.Buffered(1))
        for v in amplitudes
    ]
    return pl.pallas_call(
        functools.partial(product_kernel, counts, lo),
        grid_spec=pltpu.PrefetchScalarGridSpec(
            num_scalar_prefetch=1,
            grid=(hi - lo,),
            in_specs=whole + specs + ([] if out is None else [pl.BlockSpec(memory_space=pl.ANY)]),
            out_specs=pl.BlockSpec((rows, TILE), lambda n, place: (0, n + skip)),
            scratch_shapes=[pltpu.VMEM((rows, depth), jnp.bfloat16)] * 2,
        ),
        out_shape=jax.ShapeDtypeStruct((rows, columns), jnp.float32),
        input_output_aliases={} if out is None else {1 + len(whole) + len(specs): 0},
        compiler_params=pltpu.CompilerParams(vmem_limit_bytes=60 << 20),
        cost_estimate=pl.CostEstimate(
            flops=6 * rows * depth * count,
            bytes_accessed=4 * (rows * depth + depth * count + rows * count),
            transcendentals=0,
        ),
    )(place, *amplitudes, *[v for q in quarters for v in q], *([] if out is None else [out]))


def place_kernel(at_ref, first_ref, second_ref, out_ref):
    kept = out_ref.shape[1] // GROUP - first_ref.shape[2]
    other = pl.program_id(1) == 0

    @pl.when(other)
    def _():
        for s in range(GROUP):
            start = s * (kept + first_ref.shape[2])
            out_ref[:, start : start + kept] = second_ref[s, :, :kept]
            out_ref[:, start + kept : start + kept + first_ref.shape[2]] = first_ref[s]

    @pl.when(jnp.logical_not(other))
    def _():
        width = second_ref.shape[2] - kept
        for s in range(GROUP):
            out_ref[:, s * width : (s + 1) * width] = second_ref[s, :, kept:]


def place(at, first, second):
    sources, rows, _ = first.shape
    width = (first.shape[2] + second.shape[2]) // 2
    steps = sources // GROUP
    return pl.pallas_call(
        place_kernel,
        grid_spec=pltpu.PrefetchScalarGridSpec(
            num_scalar_prefetch=1,
            grid=(steps, 2),
            in_specs=[
                pl.BlockSpec((GROUP, rows, v.shape[2]), lambda g, i, at: (g, 0, 0))
                for v in (first, second)
            ],
            out_specs=pl.BlockSpec(
                (rows, GROUP * width), lambda g, i, at: (0, lax.rem(at[0] + 1 + i, 2) * steps + g)
            ),
        ),
        out_shape=jax.ShapeDtypeStruct((rows, 2 * sources * width), jnp.float32),
        compiler_params=pltpu.CompilerParams(vmem_limit_bytes=24 << 20),
        cost_estimate=pl.CostEstimate(
            flops=0, bytes_accessed=16 * sources * rows * width, transcendentals=0
        ),
    )(at, first, second)


def after(value, *others):
    return lax.optimization_barrier((value, *others))[0]


def on_device(amplitudes, integrals):
    x, yl, yh, core = (lax.axis_index(name) for name in ("x", "yl", "yh", "core"))
    rows, depth = amplitudes.shape
    columns = integrals.shape[1]
    half = depth // 2
    spot = jnp.stack([2 * yh + core, x])

    turns = [shift_x(amplitudes[:, half:], -d) for d in (1, 2, 3)]
    last = jnp.concatenate([amplitudes[:, half:]] + turns)
    here = jnp.broadcast_to(after(amplitudes[:, :half], last)[None], (8, rows, half))
    here = lax.all_to_all(here, "z", split_axis=0, concat_axis=0, tiled=True)
    last = lax.all_gather(last, "z", axis=0).reshape(8, 4, rows, half)
    ahead, behind = shift_x(here, -1), shift_x(here, 1)
    low, high = shift_x(ahead[:4], -1), shift_x(behind[4:], 1)
    t = (here, ahead, low, high, behind, last)

    own = integrals.T
    near, far = after((swap_near(own), swap_far(own)), low, high)
    across = [swap_far(near[: CUT * TILE]), swap_near(far[CUT * TILE :])]
    pieces = [[near], [swap_core(near)], [far], [swap_core(far)]]

    def exchange(v):
        return lax.all_to_all(
            v.reshape(-1, rows, v.shape[1]), ("x", "z"), split_axis=0, concat_axis=0, tiled=True
        )

    first = product(spot, t, pieces, tiles=(CUT, pl.cdiv(columns, TILE)))
    t = after(t, first)
    second = product(spot, t, pieces, tiles=(0, CUT), columns=CUT * TILE + columns)
    first = exchange(first)
    own2, across2 = swap_core(own), [swap_core(v) for v in across]
    second = product(spot, t, [[own], [own2], across, across2], out=second)
    first, second, at = lax.optimization_barrier((first, second, yl.reshape(1)))
    return place(at, first, exchange(second))


def solution(mesh):
    grid = Mesh(mesh.devices.reshape(2, 4, 8, 2, 2), AXES)
    return jax.shard_map(
        on_device,
        mesh=grid,
        in_specs=(P(AXES, None), P(("yh", "core"), ("yl", "x", "z"))),
        out_specs=P(AXES, None),
        check_vma=False,
    )
```

```python
import functools
import math

import jax
import jax.numpy as jnp
from jax import lax
from jax.experimental import pallas as pl
from jax.experimental.pallas import tpu as pltpu
from jax.sharding import Mesh, PartitionSpec as P

AXES = ("yl", "x", "z", "yh", "core")
TILE = 256
CUT = 3
GROUP = 16


def swap_core(value):
    return lax.ppermute(value, "core", [(0, 1), (1, 0)])


def shift_x(value, by):
    return lax.ppermute(value, "x", [(i, (i + by) % 4) for i in range(4)])


def swap_near(value):
    return lax.ppermute(value, "yl", [(0, 1), (1, 0)])


def swap_far(value):
    return lax.ppermute(value, ("yl", "yh"), [(2, 1), (1, 2), (3, 0), (0, 3)])


def halves(value):
    top = value.astype(jnp.bfloat16)
    rest = (value - top.astype(jnp.float32)).astype(jnp.bfloat16)
    return top, rest


def load_amplitudes(place_ref, first_refs, last_ref, top_ref, rest_ref):
    here_ref, ahead_ref, low_ref, high_ref, behind_ref = first_refs
    own, x = place_ref[0], place_ref[1]
    heights, _, rows, half = last_ref.shape
    part = half // 2

    @pl.loop(0, 4 * heights)
    def _(i):
        q, there = i // heights, lax.rem(i, heights)
        source = own ^ q
        take = pl.ds(pl.multiple_of((source & 1) * part, part), part)
        into = pl.ds(pl.multiple_of(q * part, part), part)
        below = there < heights // 2
        opposite = jnp.where(
            below,
            low_ref[jnp.minimum(there, heights // 2 - 1), :, take],
            high_ref[jnp.maximum(there - heights // 2, 0), :, take],
        )
        first = [here_ref[there, :, take], ahead_ref[there, :, take], opposite, behind_ref[there, :, take]]
        for d in range(4):
            value = jnp.where(source < 2, first[d], last_ref[there, d, :, take])
            row = lax.rem(x + d, 4) * (heights * rows) + there * rows
            into_rows = pl.ds(pl.multiple_of(row, rows), rows)
            top_ref[into_rows, into], rest_ref[into_rows, into] = halves(value)


def product_kernel(counts, lo, place_ref, *refs):
    pieces = refs[6 : 6 + sum(len(tiles) for tiles in counts)]
    out_ref, top_ref, rest_ref = refs[-3:]

    @pl.when(pl.program_id(0) == 0)
    def _():
        load_amplitudes(place_ref, refs[:5], refs[5], top_ref, rest_ref)

    dot = functools.partial(
        lax.dot_general,
        dimension_numbers=(((1,), (1,)), ((), ())),
        preferred_element_type=jnp.float32,
    )
    total, at = None, 0
    for q, tiles in enumerate(counts):
        value, start = pieces[at][...], tiles[0] - lo
        for i, count in enumerate(tiles[1:]):
            value = jnp.where(pl.program_id(0) < start, value, pieces[at + 1 + i][...])
            start += count
        at += len(tiles)
        top, rest = halves(value)
        depth = pl.ds(q * value.shape[1], value.shape[1])
        t_top, t_rest = top_ref[:, depth], rest_ref[:, depth]
        term = dot(t_top, rest) + dot(t_rest, top) + dot(t_top, top)
        total = term if total is None else total + term
    out_ref[...] = 0.5 * total


def product(place, amplitudes, quarters, tiles=None, columns=None, out=None):
    last = amplitudes[-1]
    rows, depth = math.prod(last.shape[:3]), 2 * last.shape[3]
    part = depth // 4
    whole_count = sum(piece.shape[0] for piece in quarters[0])
    lo, hi = tiles or (0, pl.cdiv(whole_count, TILE))
    count = min(hi * TILE, whole_count) - lo * TILE
    columns = out.shape[1] if out is not None else columns or count
    skip = (columns - count) // TILE if out is not None else 0
    specs, counts = [], []
    for quarter in quarters:
        start, sizes = -lo, []
        for piece in quarter:
            size = pl.cdiv(piece.shape[0], TILE)
            specs.append(
                pl.BlockSpec(
                    (TILE, part),
                    lambda n, place, start=start, size=size: (jnp.clip(n - start, 0, size - 1), 0),
                )
            )
            sizes.append(size)
            start += size
        counts.append(sizes)
    whole = [
        pl.BlockSpec(v.shape, lambda n, place, v=v: (0,) * v.ndim, pipeline_mode=pl.Buffered(1))
        for v in amplitudes
    ]
    return pl.pallas_call(
        functools.partial(product_kernel, counts, lo),
        grid_spec=pltpu.PrefetchScalarGridSpec(
            num_scalar_prefetch=1,
            grid=(hi - lo,),
            in_specs=whole + specs + ([] if out is None else [pl.BlockSpec(memory_space=pl.ANY)]),
            out_specs=pl.BlockSpec((rows, TILE), lambda n, place: (0, n + skip)),
            scratch_shapes=[pltpu.VMEM((rows, depth), jnp.bfloat16)] * 2,
        ),
        out_shape=jax.ShapeDtypeStruct((rows, columns), jnp.float32),
        input_output_aliases={} if out is None else {1 + len(whole) + len(specs): 0},
        compiler_params=pltpu.CompilerParams(vmem_limit_bytes=60 << 20),
        cost_estimate=pl.CostEstimate(
            flops=6 * rows * depth * count,
            bytes_accessed=4 * (rows * depth + depth * count + rows * count),
            transcendentals=0,
        ),
    )(place, *amplitudes, *[v for q in quarters for v in q], *([] if out is None else [out]))


def place_kernel(count, at_ref, *refs):
    blocks, out_ref = refs[:count], refs[-1]
    width = sum(ref.shape[2] for ref in blocks)
    for s in range(GROUP):
        start = s * width
        for ref in blocks:
            out_ref[:, start : start + ref.shape[2]] = ref[s]
            start += ref.shape[2]


def place(at, blocks, out=None):
    sources, rows, _ = blocks[0].shape
    width = sum(block.shape[2] for block in blocks)
    steps = sources // GROUP
    count = len(blocks)
    return pl.pallas_call(
        functools.partial(place_kernel, count),
        grid_spec=pltpu.PrefetchScalarGridSpec(
            num_scalar_prefetch=1,
            grid=(steps,),
            in_specs=[
                pl.BlockSpec((GROUP, rows, block.shape[2]), lambda g, at: (g, 0, 0))
                for block in blocks
            ]
            + ([] if out is None else [pl.BlockSpec(memory_space=pl.ANY)]),
            out_specs=pl.BlockSpec((rows, GROUP * width), lambda g, at: (0, at[0] * steps + g)),
        ),
        out_shape=jax.ShapeDtypeStruct((rows, 2 * sources * width), jnp.float32),
        input_output_aliases={} if out is None else {1 + count: 0},
        compiler_params=pltpu.CompilerParams(vmem_limit_bytes=16 << 20),
        cost_estimate=pl.CostEstimate(
            flops=0, bytes_accessed=8 * sources * rows * width, transcendentals=0
        ),
    )(at, *blocks, *([] if out is None else [out]))


def after(value, *others):
    return lax.optimization_barrier((value, *others))[0]


def on_device(amplitudes, integrals):
    x, yl, yh, core = (lax.axis_index(name) for name in ("x", "yl", "yh", "core"))
    rows, depth = amplitudes.shape
    columns = integrals.shape[1]
    half = depth // 2
    spot = jnp.stack([2 * yh + core, x])

    turns = [shift_x(amplitudes[:, half:], -d) for d in (1, 2, 3)]
    last = jnp.concatenate([amplitudes[:, half:]] + turns)
    here = jnp.broadcast_to(after(amplitudes[:, :half], last)[None], (8, rows, half))
    here = lax.all_to_all(here, "z", split_axis=0, concat_axis=0, tiled=True)
    last = lax.all_gather(last, "z", axis=0).reshape(8, 4, rows, half)
    ahead, behind = shift_x(here, -1), shift_x(here, 1)
    low, high = shift_x(ahead[:4], -1), shift_x(behind[4:], 1)
    t = (here, ahead, low, high, behind, last)

    own = integrals.T
    near, far = after((swap_near(own), swap_far(own)), low, high)
    pieces = [[near], [swap_core(near)], [far], [swap_core(far)]]

    def exchange(v):
        return lax.all_to_all(
            v.reshape(-1, rows, v.shape[1]), ("x", "z"), split_axis=0, concat_axis=0, tiled=True
        )

    first = product(spot, t, pieces, tiles=(CUT, pl.cdiv(columns, TILE)))
    t, own, near, far = after((t, own, near, far), first)
    across = [swap_far(near[: CUT * TILE]), swap_near(far[CUT * TILE :])]
    second = product(spot, t, pieces, tiles=(0, CUT))
    first = exchange(first)
    second = exchange(after(second, first))
    own2, across2 = swap_core(own), [swap_core(v) for v in across]
    own_block = product(spot, t, [[own], [own2], across, across2])
    out = place((1 - yl).reshape(1), [second, first])
    own_block, out, at = lax.optimization_barrier((own_block, out, yl.reshape(1)))
    return place(at, [exchange(own_block)], out)


def solution(mesh):
    grid = Mesh(mesh.devices.reshape(2, 4, 8, 2, 2), AXES)
    return jax.shard_map(
        on_device,
        mesh=grid,
        in_specs=(P(AXES, None), P(("yh", "core"), ("yl", "x", "z"))),
        out_specs=P(AXES, None),
        check_vma=False,
    )
```

```python
import functools
import math

import jax
import jax.numpy as jnp
from jax import lax
from jax.experimental import pallas as pl
from jax.experimental.pallas import tpu as pltpu
from jax.sharding import Mesh, PartitionSpec as P

AXES = ("yl", "x", "z", "yh", "core")
TILE = 256
CUT = 768
ORDER = (3, 5, 1, 7, 2, 6, 4)
GROUP = 16


def swap_core(value):
    return lax.ppermute(value, "core", [(0, 1), (1, 0)])


def shift_x(value, by):
    return lax.ppermute(value, "x", [(i, (i + by) % 4) for i in range(4)])


def shift_z(value, by):
    return lax.ppermute(value, "z", [(i, (i + by) % 8) for i in range(8)])


def swap_near(value):
    return lax.ppermute(value, "yl", [(0, 1), (1, 0)])


def swap_far(value):
    return lax.ppermute(value, ("yl", "yh"), [(2, 1), (1, 2), (3, 0), (0, 3)])


def halves(value):
    top = value.astype(jnp.bfloat16)
    rest = (value - top.astype(jnp.float32)).astype(jnp.bfloat16)
    return top, rest


def load_amplitudes(place_ref, around, first_refs, last_ref, top_ref, rest_ref):
    here_ref, ahead_ref, low_ref, high_ref, behind_ref = first_refs
    own, x, z = place_ref[0], place_ref[1], place_ref[2]
    heights, _, rows, half = last_ref.shape
    part = half // 2

    @pl.loop(0, 4 * heights)
    def _(i):
        q, there = i // heights, lax.rem(i, heights)
        source = own ^ q
        take = pl.ds(pl.multiple_of((source & 1) * part, part), part)
        into = pl.ds(pl.multiple_of(q * part, part), part)
        below = there < heights // 2
        opposite = jnp.where(
            below,
            low_ref[jnp.minimum(there, heights // 2 - 1), :, take],
            high_ref[jnp.maximum(there - heights // 2, 0), :, take],
        )
        first = [here_ref[there, :, take], ahead_ref[there, :, take], opposite, behind_ref[there, :, take]]
        for d in range(4):
            value = jnp.where(source < 2, first[d], last_ref[there, d, :, take])
            if around:
                row = lax.rem(there - z + heights, heights) * (4 * rows) + d * rows
            else:
                row = lax.rem(x + d, 4) * (heights * rows) + there * rows
            into_rows = pl.ds(pl.multiple_of(row, rows), rows)
            top_ref[into_rows, into], rest_ref[into_rows, into] = halves(value)


def product_kernel(around, counts, place_ref, *refs):
    pieces = refs[6 : 6 + sum(len(tiles) for tiles in counts)]
    outs, (top_ref, rest_ref) = refs[6 + len(pieces) : -2], refs[-2:]

    @pl.when(pl.program_id(0) == 0)
    def _():
        load_amplitudes(place_ref, around, refs[:5], refs[5], top_ref, rest_ref)

    dot = functools.partial(
        lax.dot_general,
        dimension_numbers=(((1,), (1,)), ((), ())),
        preferred_element_type=jnp.float32,
    )
    total, at = None, 0
    for q, tiles in enumerate(counts):
        value, start = pieces[at][...], tiles[0]
        for i, count in enumerate(tiles[1:]):
            value = jnp.where(pl.program_id(0) < start, value, pieces[at + 1 + i][...])
            start += count
        at += len(tiles)
        top, rest = halves(value)
        depth = pl.ds(q * value.shape[1], value.shape[1])
        t_top, t_rest = top_ref[:, depth], rest_ref[:, depth]
        term = dot(t_top, rest) + dot(t_rest, top) + dot(t_top, top)
        total = term if total is None else total + term
    count = total.shape[0] // len(outs)
    for i, out_ref in enumerate(outs):
        out_ref[...] = 0.5 * total[i * count : (i + 1) * count]


def product(place, amplitudes, quarters, around=False):
    last = amplitudes[-1]
    rows, depth = math.prod(last.shape[:3]), 2 * last.shape[3]
    part = depth // 4
    outs = last.shape[0] if around else 1
    columns = sum(piece.shape[0] for piece in quarters[0])
    specs, counts = [], []
    for quarter in quarters:
        start, tiles = 0, []
        for piece in quarter:
            count = pl.cdiv(piece.shape[0], TILE)
            specs.append(
                pl.BlockSpec(
                    (TILE, part),
                    lambda n, place, start=start, count=count: (jnp.clip(n - start, 0, count - 1), 0),
                )
            )
            tiles.append(count)
            start += count
        counts.append(tiles)
    whole = [
        pl.BlockSpec(v.shape, lambda n, place, v=v: (0,) * v.ndim, pipeline_mode=pl.Buffered(1))
        for v in amplitudes
    ]
    return pl.pallas_call(
        functools.partial(product_kernel, around, counts),
        grid_spec=pltpu.PrefetchScalarGridSpec(
            num_scalar_prefetch=1,
            grid=(pl.cdiv(columns, TILE),),
            in_specs=whole + specs,
            out_specs=[pl.BlockSpec((rows // outs, TILE), lambda n, place: (0, n))] * outs,
            scratch_shapes=[pltpu.VMEM((rows, depth), jnp.bfloat16)] * 2,
        ),
        out_shape=[jax.ShapeDtypeStruct((rows // outs, columns), jnp.float32)] * outs,
        compiler_params=pltpu.CompilerParams(vmem_limit_bytes=60 << 20),
        cost_estimate=pl.CostEstimate(
            flops=6 * rows * depth * columns,
            bytes_accessed=4 * (rows * depth + depth * columns + rows * columns),
            transcendentals=0,
        ),
    )(place, *amplitudes, *[piece for quarter in quarters for piece in quarter])


def regroup_kernel(chunks, z_ref, *refs):
    heights = len(refs[: -4]) // chunks
    outs = refs[-4:]
    for e in range(heights):
        source = lax.rem(z_ref[0] - e + heights, heights)
        at = 0
        for c in range(chunks):
            piece_ref = refs[c * heights + e]
            width = piece_ref.shape[2]
            for d, out_ref in enumerate(outs):
                out_ref[source, :, at : at + width] = piece_ref[d]
            at += width


def regroup(z, chunks):
    heights = len(chunks[0])
    _, rows, _ = chunks[0][0].shape
    width = sum(chunk[0].shape[2] for chunk in chunks)
    pieces = [piece for chunk in chunks for piece in chunk]
    return pl.pallas_call(
        functools.partial(regroup_kernel, len(chunks)),
        grid_spec=pltpu.PrefetchScalarGridSpec(
            num_scalar_prefetch=1,
            grid=(1,),
            in_specs=[pl.BlockSpec(v.shape, lambda n, z: (0, 0, 0)) for v in pieces],
            out_specs=[pl.BlockSpec((heights, rows, width), lambda n, z: (0, 0, 0))] * 4,
        ),
        out_shape=[jax.ShapeDtypeStruct((heights, rows, width), jnp.float32)] * 4,
        compiler_params=pltpu.CompilerParams(vmem_limit_bytes=32 << 20),
        cost_estimate=pl.CostEstimate(
            flops=0, bytes_accessed=32 * heights * rows * width, transcendentals=0
        ),
    )(z, *pieces)


def place_kernel(at_ref, block_ref, _, out_ref):
    width = block_ref.shape[2]
    for s in range(GROUP):
        out_ref[:, s * width : (s + 1) * width] = block_ref[s]


def place(at, block, out):
    sources, rows, width = block.shape
    steps = sources // GROUP
    return pl.pallas_call(
        place_kernel,
        grid_spec=pltpu.PrefetchScalarGridSpec(
            num_scalar_prefetch=1,
            grid=(steps,),
            in_specs=[
                pl.BlockSpec((GROUP, rows, width), lambda g, at: (g, 0, 0)),
                pl.BlockSpec(memory_space=pl.ANY),
            ],
            out_specs=pl.BlockSpec((rows, GROUP * width), lambda g, at: (0, at[0] * steps + g)),
        ),
        out_shape=jax.ShapeDtypeStruct(out.shape, jnp.float32),
        input_output_aliases={2: 0},
        compiler_params=pltpu.CompilerParams(vmem_limit_bytes=16 << 20),
        cost_estimate=pl.CostEstimate(
            flops=0, bytes_accessed=8 * sources * rows * width, transcendentals=0
        ),
    )(at, block, out)


def place_by_x_kernel(at_ref, *refs):
    blocks, out_ref, by_source_ref = refs[:-2], refs[-2], refs[-1]
    heights, _, width = blocks[0].shape

    @pl.when(pl.program_id(0) == 0)
    def _():
        for d, ref in enumerate(blocks):
            source = lax.rem(at_ref[1] - d + 4, 4) * heights

            @pl.loop(0, heights)
            def _(s, ref=ref, source=source):
                by_source_ref[source + s] = ref[s]

    for s in range(GROUP):
        out_ref[:, s * width : (s + 1) * width] = by_source_ref[pl.program_id(0) * GROUP + s]


def place_by_x(at, blocks):
    heights, rows, width = blocks[0].shape
    steps = 4 * heights // GROUP
    return pl.pallas_call(
        place_by_x_kernel,
        grid_spec=pltpu.PrefetchScalarGridSpec(
            num_scalar_prefetch=1,
            grid=(steps,),
            in_specs=[pl.BlockSpec((heights, rows, width), lambda g, at: (0, 0, 0))] * 4,
            out_specs=pl.BlockSpec((rows, GROUP * width), lambda g, at: (0, at[0] * steps + g)),
            scratch_shapes=[pltpu.VMEM((4 * heights, rows, width), jnp.float32)],
        ),
        out_shape=jax.ShapeDtypeStruct((rows, 8 * heights * width), jnp.float32),
        compiler_params=pltpu.CompilerParams(vmem_limit_bytes=32 << 20),
        cost_estimate=pl.CostEstimate(
            flops=0, bytes_accessed=32 * heights * rows * width, transcendentals=0
        ),
    )(at, *blocks)


def after(value, *others):
    return lax.optimization_barrier((value, *others))[0]


def on_device(amplitudes, integrals):
    x, z, yl, yh, core = (lax.axis_index(name) for name in ("x", "z", "yl", "yh", "core"))
    rows, depth = amplitudes.shape
    columns = integrals.shape[1]
    half = depth // 2
    spot = jnp.stack([2 * yh + core, x, z])

    turns = [shift_x(amplitudes[:, half:], -d) for d in (1, 2, 3)]
    last = jnp.concatenate([amplitudes[:, half:]] + turns)
    here = jnp.broadcast_to(after(amplitudes[:, :half], last)[None], (8, rows, half))
    here = lax.all_to_all(here, "z", split_axis=0, concat_axis=0, tiled=True)
    own2 = swap_core(integrals.T)
    here = after(here, own2)
    last = lax.all_gather(last, "z", axis=0).reshape(8, 4, rows, half)
    ahead, behind = shift_x(here, -1), shift_x(here, 1)
    low, high = shift_x(ahead[:4], -1), shift_x(behind[4:], 1)
    t = (here, ahead, low, high, behind, last)

    own = integrals.T
    near, far = after((swap_near(own), swap_far(own)), low, high)
    across = [swap_far(near[:CUT]), swap_near(far[CUT:])]
    results = product(spot, t, [[near], [swap_core(near)], [far], [swap_core(far)]], around=True)
    sent = {e: shift_z(results[e], e) for e in ORDER}
    across = after(across, sent[3], sent[5])
    across2 = [swap_core(v) for v in across]
    t = after(t, sent[3], sent[5])
    (own_block,) = product(spot, t, [[own], [own2], across, across2])
    own_block = after(own_block, *sent.values())
    own_block = lax.all_to_all(
        own_block.reshape(32, rows, columns), ("x", "z"), split_axis=0, concat_axis=0, tiled=True
    )
    chunks = [[v.reshape(4, rows, columns) for v in [results[0]] + [sent[e] for e in range(1, 8)]]]
    by_x = regroup(z.reshape(1), chunks)
    by_x = [by_x[0]] + [shift_x(by_x[d], d) for d in (1, 2, 3)]
    out = place_by_x(jnp.stack([1 - yl, x]), by_x)
    return place(yl.reshape(1), own_block, out)


def solution(mesh):
    grid = Mesh(mesh.devices.reshape(2, 4, 8, 2, 2), AXES)
    return jax.shard_map(
        on_device,
        mesh=grid,
        in_specs=(P(AXES, None), P(("yh", "core"), ("yl", "x", "z"))),
        out_specs=P(AXES, None),
        check_vma=False,
    )
```

```python
import functools
import math

import jax
import jax.numpy as jnp
from jax import lax
from jax.experimental import pallas as pl
from jax.experimental.pallas import tpu as pltpu
from jax.sharding import Mesh, PartitionSpec as P

AXES = ("yl", "x", "z", "yh", "core")
TILE = 256
CUT = 768
GROUP = 16


def swap_core(value):
    return lax.ppermute(value, "core", [(0, 1), (1, 0)])


def shift_x(value, by):
    return lax.ppermute(value, "x", [(i, (i + by) % 4) for i in range(4)])


def swap_near(value):
    return lax.ppermute(value, "yl", [(0, 1), (1, 0)])


def swap_far(value):
    return lax.ppermute(value, ("yl", "yh"), [(2, 1), (1, 2), (3, 0), (0, 3)])


def halves(value):
    top = value.astype(jnp.bfloat16)
    rest = (value - top.astype(jnp.float32)).astype(jnp.bfloat16)
    return top, rest


def load_amplitudes(place_ref, around, first_refs, last_ref, top_ref, rest_ref):
    here_ref, ahead_ref, low_ref, high_ref, behind_ref = first_refs
    own, x, z = place_ref[0], place_ref[1], place_ref[2]
    heights, _, rows, half = last_ref.shape
    part = half // 2

    @pl.loop(0, 4 * heights)
    def _(i):
        q, there = i // heights, lax.rem(i, heights)
        source = own ^ q
        take = pl.ds(pl.multiple_of((source & 1) * part, part), part)
        into = pl.ds(pl.multiple_of(q * part, part), part)
        below = there < heights // 2
        opposite = jnp.where(
            below,
            low_ref[jnp.minimum(there, heights // 2 - 1), :, take],
            high_ref[jnp.maximum(there - heights // 2, 0), :, take],
        )
        first = [here_ref[there, :, take], ahead_ref[there, :, take], opposite, behind_ref[there, :, take]]
        for d in range(4):
            value = jnp.where(source < 2, first[d], last_ref[there, d, :, take])
            if around:
                row = lax.rem(there - z + heights, heights) * (4 * rows) + d * rows
            else:
                row = lax.rem(x + d, 4) * (heights * rows) + there * rows
            into_rows = pl.ds(pl.multiple_of(row, rows), rows)
            top_ref[into_rows, into], rest_ref[into_rows, into] = halves(value)


def product_kernel(around, counts, place_ref, *refs):
    pieces = refs[6 : 6 + sum(len(tiles) for tiles in counts)]
    outs, (top_ref, rest_ref) = refs[6 + len(pieces) : -2], refs[-2:]

    @pl.when(pl.program_id(0) == 0)
    def _():
        load_amplitudes(place_ref, around, refs[:5], refs[5], top_ref, rest_ref)

    dot = functools.partial(
        lax.dot_general,
        dimension_numbers=(((1,), (1,)), ((), ())),
        preferred_element_type=jnp.float32,
    )
    total, at = None, 0
    for q, tiles in enumerate(counts):
        value, start = pieces[at][...], tiles[0]
        for i, count in enumerate(tiles[1:]):
            value = jnp.where(pl.program_id(0) < start, value, pieces[at + 1 + i][...])
            start += count
        at += len(tiles)
        top, rest = halves(value)
        depth = pl.ds(q * value.shape[1], value.shape[1])
        t_top, t_rest = top_ref[:, depth], rest_ref[:, depth]
        term = dot(t_top, rest) + dot(t_rest, top) + dot(t_top, top)
        total = term if total is None else total + term
    count = total.shape[0] // len(outs)
    for i, out_ref in enumerate(outs):
        out_ref[...] = 0.5 * total[i * count : (i + 1) * count]


def product(place, amplitudes, quarters, around=False):
    last = amplitudes[-1]
    rows, depth = math.prod(last.shape[:3]), 2 * last.shape[3]
    part = depth // 4
    outs = last.shape[0] if around else 1
    columns = sum(piece.shape[0] for piece in quarters[0])
    specs, counts = [], []
    for quarter in quarters:
        start, tiles = 0, []
        for piece in quarter:
            count = pl.cdiv(piece.shape[0], TILE)
            specs.append(
                pl.BlockSpec(
                    (TILE, part),
                    lambda n, place, start=start, count=count: (jnp.clip(n - start, 0, count - 1), 0),
                )
            )
            tiles.append(count)
            start += count
        counts.append(tiles)
    whole = [
        pl.BlockSpec(v.shape, lambda n, place, v=v: (0,) * v.ndim, pipeline_mode=pl.Buffered(1))
        for v in amplitudes
    ]
    return pl.pallas_call(
        functools.partial(product_kernel, around, counts),
        grid_spec=pltpu.PrefetchScalarGridSpec(
            num_scalar_prefetch=1,
            grid=(pl.cdiv(columns, TILE),),
            in_specs=whole + specs,
            out_specs=[pl.BlockSpec((rows // outs, TILE), lambda n, place: (0, n))] * outs,
            scratch_shapes=[pltpu.VMEM((rows, depth), jnp.bfloat16)] * 2,
        ),
        out_shape=[jax.ShapeDtypeStruct((rows // outs, columns), jnp.float32)] * outs,
        compiler_params=pltpu.CompilerParams(vmem_limit_bytes=60 << 20),
        cost_estimate=pl.CostEstimate(
            flops=6 * rows * depth * columns,
            bytes_accessed=4 * (rows * depth + depth * columns + rows * columns),
            transcendentals=0,
        ),
    )(place, *amplitudes, *[piece for quarter in quarters for piece in quarter])


def place_kernel(count, at_ref, *refs):
    blocks, out_ref = refs[:count], refs[-1]
    width = sum(ref.shape[2] for ref in blocks)
    for s in range(GROUP):
        start = s * width
        for ref in blocks:
            out_ref[:, start : start + ref.shape[2]] = ref[s]
            start += ref.shape[2]


def place(at, blocks, out=None):
    sources, rows, _ = blocks[0].shape
    width = sum(block.shape[2] for block in blocks)
    steps = sources // GROUP
    count = len(blocks)
    return pl.pallas_call(
        functools.partial(place_kernel, count),
        grid_spec=pltpu.PrefetchScalarGridSpec(
            num_scalar_prefetch=1,
            grid=(steps,),
            in_specs=[
                pl.BlockSpec((GROUP, rows, block.shape[2]), lambda g, at: (g, 0, 0))
                for block in blocks
            ]
            + ([] if out is None else [pl.BlockSpec(memory_space=pl.ANY)]),
            out_specs=pl.BlockSpec((rows, GROUP * width), lambda g, at: (0, at[0] * steps + g)),
        ),
        out_shape=jax.ShapeDtypeStruct((rows, 2 * sources * width), jnp.float32),
        input_output_aliases={} if out is None else {1 + count: 0},
        compiler_params=pltpu.CompilerParams(vmem_limit_bytes=16 << 20),
        cost_estimate=pl.CostEstimate(
            flops=0, bytes_accessed=8 * sources * rows * width, transcendentals=0
        ),
    )(at, *blocks, *([] if out is None else [out]))


def after(value, *others):
    return lax.optimization_barrier((value, *others))[0]


def on_device(amplitudes, integrals):
    x, z, yl, yh, core = (lax.axis_index(name) for name in ("x", "z", "yl", "yh", "core"))
    rows, depth = amplitudes.shape
    columns = integrals.shape[1]
    half = depth // 2
    spot = jnp.stack([2 * yh + core, x, z])

    turns = [shift_x(amplitudes[:, half:], -d) for d in (1, 2, 3)]
    last = jnp.concatenate([amplitudes[:, half:]] + turns)
    here = jnp.broadcast_to(after(amplitudes[:, :half], last)[None], (8, rows, half))
    here = lax.all_to_all(here, "z", split_axis=0, concat_axis=0, tiled=True)
    last = lax.all_gather(last, "z", axis=0).reshape(8, 4, rows, half)
    ahead, behind = shift_x(here, -1), shift_x(here, 1)
    low, high = shift_x(ahead[:4], -1), shift_x(behind[4:], 1)
    t = (here, ahead, low, high, behind, last)

    first, second = integrals.T[:CUT], integrals.T[CUT:]
    near = swap_near(after(first, ahead, behind))
    far = swap_far(after(first, low, high))
    near_next, far_next = after((swap_near(second), swap_far(second)), ahead, behind)

    def exchange(v):
        return lax.all_to_all(
            v.reshape(-1, rows, v.shape[1]), ("x", "z"), split_axis=0, concat_axis=0, tiled=True
        )

    (result,) = product(spot, t, [[near], [swap_core(near)], [far], [swap_core(far)]])
    (result_next,) = product(
        spot, t, [[near_next], [swap_core(near_next)], [far_next], [swap_core(far_next)]]
    )
    other_block = [exchange(result), exchange(result_next)]
    across = [swap_far(near), swap_near(far_next)]
    own, own2, across2 = [first, second], [swap_core(first), swap_core(second)], [swap_core(v) for v in across]
    (own_block,) = product(spot, t, [own, own2, across, across2])
    own_block = exchange(after(own_block, other_block[1]))
    out = place((1 - yl).reshape(1), other_block)
    return place(yl.reshape(1), [own_block], out)


def solution(mesh):
    grid = Mesh(mesh.devices.reshape(2, 4, 8, 2, 2), AXES)
    return jax.shard_map(
        on_device,
        mesh=grid,
        in_specs=(P(AXES, None), P(("yh", "core"), ("yl", "x", "z"))),
        out_specs=P(AXES, None),
        check_vma=False,
    )
```

```python
import functools
import math

import jax
import jax.numpy as jnp
from jax import lax
from jax.experimental import pallas as pl
from jax.experimental.pallas import tpu as pltpu
from jax.sharding import Mesh, PartitionSpec as P

AXES = ("yl", "x", "z", "yh", "core")
TILE = 256
CUT = 768
GROUP = 16


def swap_core(value):
    return lax.ppermute(value, "core", [(0, 1), (1, 0)])


def shift_x(value, by):
    return lax.ppermute(value, "x", [(i, (i + by) % 4) for i in range(4)])


def swap_near(value):
    return lax.ppermute(value, "yl", [(0, 1), (1, 0)])


def swap_far(value):
    return lax.ppermute(value, ("yl", "yh"), [(2, 1), (1, 2), (3, 0), (0, 3)])


def halves(value):
    top = value.astype(jnp.bfloat16)
    rest = (value - top.astype(jnp.float32)).astype(jnp.bfloat16)
    return top, rest


def load_amplitudes(place_ref, pieces, last_ref, top_ref, rest_ref):
    own, x = place_ref[0], place_ref[1]
    part = last_ref.shape[3]

    @pl.loop(0, 4)
    def _(q):
        source = own ^ q
        take = pl.ds(pl.multiple_of(jnp.minimum(source, 2) * part, part), part)
        into = pl.ds(pl.multiple_of(q * part, part), part)
        for d, refs in enumerate(pieces):
            last = last_ref[:, d].reshape(-1, part)
            row = lax.rem(x + d, 4) * last.shape[0]
            at = 0
            for ref in refs:
                count = ref.shape[0]
                value = jnp.where(source < 3, ref[:, take], last[at : at + count])
                rows = pl.ds(pl.multiple_of(row + at, count), count)
                top_ref[rows, into], rest_ref[rows, into] = halves(value)
                at += count


def product_kernel(counts, place_ref, *refs):
    pieces, (out_ref, top_ref, rest_ref) = refs[6:-3], refs[-3:]

    @pl.when(pl.program_id(0) == 0)
    def _():
        here, ahead, behind, low, high, last_ref = refs[:6]
        load_amplitudes(
            place_ref, [[here], [ahead], [low, high], [behind]], last_ref, top_ref, rest_ref
        )

    dot = functools.partial(
        lax.dot_general,
        dimension_numbers=(((1,), (1,)), ((), ())),
        preferred_element_type=jnp.float32,
    )
    total, at = None, 0
    for q, tiles in enumerate(counts):
        value, start = pieces[at][...], tiles[0]
        for i, count in enumerate(tiles[1:]):
            value = jnp.where(pl.program_id(0) < start, value, pieces[at + 1 + i][...])
            start += count
        at += len(tiles)
        top, rest = halves(value)
        depth = pl.ds(q * value.shape[1], value.shape[1])
        t_top, t_rest = top_ref[:, depth], rest_ref[:, depth]
        term = dot(t_top, rest) + dot(t_rest, top) + dot(t_top, top)
        total = term if total is None else total + term
    out_ref[...] = 0.5 * total


def product(place, amplitudes, quarters):
    last = amplitudes[-1]
    rows, part = math.prod(last.shape[:3]), last.shape[3]
    depth = 4 * part
    columns = sum(piece.shape[0] for piece in quarters[0])
    specs, counts = [], []
    for quarter in quarters:
        start, tiles = 0, []
        for piece in quarter:
            count = pl.cdiv(piece.shape[0], TILE)
            specs.append(
                pl.BlockSpec(
                    (TILE, part),
                    lambda n, place, start=start, count=count: (jnp.clip(n - start, 0, count - 1), 0),
                )
            )
            tiles.append(count)
            start += count
        counts.append(tiles)
    whole = [
        pl.BlockSpec(v.shape, lambda n, place, v=v: (0,) * v.ndim, pipeline_mode=pl.Buffered(1))
        for v in amplitudes
    ]
    return pl.pallas_call(
        functools.partial(product_kernel, counts),
        grid_spec=pltpu.PrefetchScalarGridSpec(
            num_scalar_prefetch=1,
            grid=(pl.cdiv(columns, TILE),),
            in_specs=whole + specs,
            out_specs=pl.BlockSpec((rows, TILE), lambda n, place: (0, n)),
            scratch_shapes=[pltpu.VMEM((rows, depth), jnp.bfloat16)] * 2,
        ),
        out_shape=jax.ShapeDtypeStruct((rows, columns), jnp.float32),
        compiler_params=pltpu.CompilerParams(vmem_limit_bytes=60 << 20),
        cost_estimate=pl.CostEstimate(
            flops=6 * rows * depth * columns,
            bytes_accessed=4 * (rows * depth + depth * columns + rows * columns),
            transcendentals=0,
        ),
    )(place, *amplitudes, *[piece for quarter in quarters for piece in quarter])


def place_kernel(count, at_ref, *refs):
    blocks, out_ref = refs[:count], refs[-1]
    width = sum(ref.shape[2] for ref in blocks)
    for s in range(GROUP):
        start = s * width
        for ref in blocks:
            out_ref[:, start : start + ref.shape[2]] = ref[s]
            start += ref.shape[2]


def place(at, blocks, out=None):
    sources, rows, _ = blocks[0].shape
    width = sum(block.shape[2] for block in blocks)
    steps = sources // GROUP
    count = len(blocks)
    return pl.pallas_call(
        functools.partial(place_kernel, count),
        grid_spec=pltpu.PrefetchScalarGridSpec(
            num_scalar_prefetch=1,
            grid=(steps,),
            in_specs=[
                pl.BlockSpec((GROUP, rows, block.shape[2]), lambda g, at: (g, 0, 0))
                for block in blocks
            ]
            + ([] if out is None else [pl.BlockSpec(memory_space=pl.ANY)]),
            out_specs=pl.BlockSpec((rows, GROUP * width), lambda g, at: (0, at[0] * steps + g)),
        ),
        out_shape=jax.ShapeDtypeStruct((rows, 2 * sources * width), jnp.float32),
        input_output_aliases={} if out is None else {1 + count: 0},
        compiler_params=pltpu.CompilerParams(vmem_limit_bytes=16 << 20),
        cost_estimate=pl.CostEstimate(
            flops=0, bytes_accessed=8 * sources * rows * width, transcendentals=0
        ),
    )(at, *blocks, *([] if out is None else [out]))


def gather_amplitudes(amplitudes):
    rows, depth = amplitudes.shape
    part = depth // 4
    last = amplitudes[:, 3 * part :]
    last = jnp.concatenate([last] + [shift_x(last, -d) for d in (1, 2, 3)])
    last = lax.all_gather(last, "z", axis=0).reshape(8, 4, rows, part)
    here = jnp.broadcast_to(amplitudes[None, :, : 3 * part], (8, rows, 3 * part))
    here = lax.all_to_all(here, "z", split_axis=0, concat_axis=0, tiled=True).reshape(-1, 3 * part)
    ahead, behind = shift_x(here, -1), shift_x(here, 1)
    return [here, ahead, behind, last]


def after(value, *others):
    return lax.optimization_barrier((value, *others))[0]


def on_device(amplitudes, integrals):
    x, yl, yh, core = (lax.axis_index(name) for name in ("x", "yl", "yh", "core"))
    rows = amplitudes.shape[0]
    columns = integrals.shape[1]
    spot = jnp.stack([2 * yh + core, x])
    here, ahead, behind, last = gather_amplitudes(amplitudes)

    own = [integrals.T[:CUT], integrals.T[CUT:]]
    near, far = [swap_near(v) for v in own], [swap_far(v) for v in own]
    across = [swap_far(near[0]), swap_near(far[1])]
    swapped = swap_core(near[1]), swap_core(far[1])
    half = here.shape[0] // 2
    low, high = shift_x(after(ahead[:half], *swapped), -1), shift_x(after(behind[half:], *swapped), 1)
    t = [here, ahead, behind, low, high, last]

    def exchange(v):
        return lax.all_to_all(
            v.reshape(-1, rows, v.shape[1]), ("x", "z"), split_axis=0, concat_axis=0, tiled=True
        )

    near2, far2 = (swap_core(near[0]), swapped[0]), (swap_core(far[0]), swapped[1])
    other_block = [
        exchange(product(spot, t, [[n], [n2], [f], [f2]]))
        for n, n2, f, f2 in zip(near, near2, far, far2)
    ]
    own2, across2 = [swap_core(v) for v in own], [swap_core(v) for v in across]
    own_block = exchange(product(spot, t, [own, own2, across, across2]))
    out = place((1 - yl).reshape(1), other_block)
    return place(yl.reshape(1), [own_block], out)


def solution(mesh):
    grid = Mesh(mesh.devices.reshape(2, 4, 8, 2, 2), AXES)
    return jax.shard_map(
        on_device,
        mesh=grid,
        in_specs=(P(AXES, None), P(("yh", "core"), ("yl", "x", "z"))),
        out_specs=P(AXES, None),
        check_vma=False,
    )
```

```python
import functools
import math

import jax
import jax.numpy as jnp
from jax import lax
from jax.experimental import pallas as pl
from jax.experimental.pallas import tpu as pltpu
from jax.sharding import Mesh, PartitionSpec as P

AXES = ("yl", "x", "z", "yh", "core")
TILE = 256
CUT = 768
GROUP = 16


def swap_core(value):
    return lax.ppermute(value, "core", [(0, 1), (1, 0)])


def shift_x(value, by):
    return lax.ppermute(value, "x", [(i, (i + by) % 4) for i in range(4)])


def swap_near(value):
    return lax.ppermute(value, "yl", [(0, 1), (1, 0)])


def swap_far(value):
    return lax.ppermute(value, ("yl", "yh"), [(2, 1), (1, 2), (3, 0), (0, 3)])


def halves(value):
    top = value.astype(jnp.bfloat16)
    rest = (value - top.astype(jnp.float32)).astype(jnp.bfloat16)
    return top, rest


def load_amplitudes(place_ref, around, first_refs, last_ref, top_ref, rest_ref):
    here_ref, ahead_ref, low_ref, high_ref, behind_ref = first_refs
    own, x, z = place_ref[0], place_ref[1], place_ref[2]
    heights, _, rows, half = last_ref.shape
    part = half // 2

    @pl.loop(0, 4 * heights)
    def _(i):
        q, there = i // heights, lax.rem(i, heights)
        source = own ^ q
        take = pl.ds(pl.multiple_of((source & 1) * part, part), part)
        into = pl.ds(pl.multiple_of(q * part, part), part)
        below = there < heights // 2
        opposite = jnp.where(
            below,
            low_ref[jnp.minimum(there, heights // 2 - 1), :, take],
            high_ref[jnp.maximum(there - heights // 2, 0), :, take],
        )
        first = [here_ref[there, :, take], ahead_ref[there, :, take], opposite, behind_ref[there, :, take]]
        for d in range(4):
            value = jnp.where(source < 2, first[d], last_ref[there, d, :, take])
            if around:
                row = lax.rem(there - z + heights, heights) * (4 * rows) + d * rows
            else:
                row = lax.rem(x + d, 4) * (heights * rows) + there * rows
            into_rows = pl.ds(pl.multiple_of(row, rows), rows)
            top_ref[into_rows, into], rest_ref[into_rows, into] = halves(value)


def product_kernel(around, counts, place_ref, *refs):
    pieces = refs[6 : 6 + sum(len(tiles) for tiles in counts)]
    outs, (top_ref, rest_ref) = refs[6 + len(pieces) : -2], refs[-2:]

    @pl.when(pl.program_id(0) == 0)
    def _():
        load_amplitudes(place_ref, around, refs[:5], refs[5], top_ref, rest_ref)

    dot = functools.partial(
        lax.dot_general,
        dimension_numbers=(((1,), (1,)), ((), ())),
        preferred_element_type=jnp.float32,
    )
    total, at = None, 0
    for q, tiles in enumerate(counts):
        value, start = pieces[at][...], tiles[0]
        for i, count in enumerate(tiles[1:]):
            value = jnp.where(pl.program_id(0) < start, value, pieces[at + 1 + i][...])
            start += count
        at += len(tiles)
        top, rest = halves(value)
        depth = pl.ds(q * value.shape[1], value.shape[1])
        t_top, t_rest = top_ref[:, depth], rest_ref[:, depth]
        term = dot(t_top, rest) + dot(t_rest, top) + dot(t_top, top)
        total = term if total is None else total + term
    count = total.shape[0] // len(outs)
    for i, out_ref in enumerate(outs):
        out_ref[...] = 0.5 * total[i * count : (i + 1) * count]


def product(place, amplitudes, quarters, around=False):
    last = amplitudes[-1]
    rows, depth = math.prod(last.shape[:3]), 2 * last.shape[3]
    part = depth // 4
    outs = last.shape[0] if around else 1
    columns = sum(piece.shape[0] for piece in quarters[0])
    specs, counts = [], []
    for quarter in quarters:
        start, tiles = 0, []
        for piece in quarter:
            count = pl.cdiv(piece.shape[0], TILE)
            specs.append(
                pl.BlockSpec(
                    (TILE, part),
                    lambda n, place, start=start, count=count: (jnp.clip(n - start, 0, count - 1), 0),
                )
            )
            tiles.append(count)
            start += count
        counts.append(tiles)
    whole = [
        pl.BlockSpec(v.shape, lambda n, place, v=v: (0,) * v.ndim, pipeline_mode=pl.Buffered(1))
        for v in amplitudes
    ]
    return pl.pallas_call(
        functools.partial(product_kernel, around, counts),
        grid_spec=pltpu.PrefetchScalarGridSpec(
            num_scalar_prefetch=1,
            grid=(pl.cdiv(columns, TILE),),
            in_specs=whole + specs,
            out_specs=[pl.BlockSpec((rows // outs, TILE), lambda n, place: (0, n))] * outs,
            scratch_shapes=[pltpu.VMEM((rows, depth), jnp.bfloat16)] * 2,
        ),
        out_shape=[jax.ShapeDtypeStruct((rows // outs, columns), jnp.float32)] * outs,
        compiler_params=pltpu.CompilerParams(vmem_limit_bytes=60 << 20),
        cost_estimate=pl.CostEstimate(
            flops=6 * rows * depth * columns,
            bytes_accessed=4 * (rows * depth + depth * columns + rows * columns),
            transcendentals=0,
        ),
    )(place, *amplitudes, *[piece for quarter in quarters for piece in quarter])


def place_kernel(count, at_ref, *refs):
    blocks, out_ref = refs[:count], refs[-1]
    width = sum(ref.shape[2] for ref in blocks)
    for s in range(GROUP):
        start = s * width
        for ref in blocks:
            out_ref[:, start : start + ref.shape[2]] = ref[s]
            start += ref.shape[2]


def place(at, blocks, out=None):
    sources, rows, _ = blocks[0].shape
    width = sum(block.shape[2] for block in blocks)
    steps = sources // GROUP
    count = len(blocks)
    return pl.pallas_call(
        functools.partial(place_kernel, count),
        grid_spec=pltpu.PrefetchScalarGridSpec(
            num_scalar_prefetch=1,
            grid=(steps,),
            in_specs=[
                pl.BlockSpec((GROUP, rows, block.shape[2]), lambda g, at: (g, 0, 0))
                for block in blocks
            ]
            + ([] if out is None else [pl.BlockSpec(memory_space=pl.ANY)]),
            out_specs=pl.BlockSpec((rows, GROUP * width), lambda g, at: (0, at[0] * steps + g)),
        ),
        out_shape=jax.ShapeDtypeStruct((rows, 2 * sources * width), jnp.float32),
        input_output_aliases={} if out is None else {1 + count: 0},
        compiler_params=pltpu.CompilerParams(vmem_limit_bytes=16 << 20),
        cost_estimate=pl.CostEstimate(
            flops=0, bytes_accessed=8 * sources * rows * width, transcendentals=0
        ),
    )(at, *blocks, *([] if out is None else [out]))


def after(value, *others):
    return lax.optimization_barrier((value, *others))[0]


def on_device(amplitudes, integrals):
    x, z, yl, yh, core = (lax.axis_index(name) for name in ("x", "z", "yl", "yh", "core"))
    rows, depth = amplitudes.shape
    columns = integrals.shape[1]
    half = depth // 2
    spot = jnp.stack([2 * yh + core, x, z])

    turns = [shift_x(amplitudes[:, half:], -d) for d in (1, 2, 3)]
    last = jnp.concatenate([amplitudes[:, half:]] + turns)
    here = jnp.broadcast_to(after(amplitudes[:, :half], last)[None], (8, rows, half))
    here = lax.all_to_all(here, "z", split_axis=0, concat_axis=0, tiled=True)
    last = lax.all_gather(last, "z", axis=0).reshape(8, 4, rows, half)
    ahead, behind = shift_x(here, -1), shift_x(here, 1)

    first, second = integrals.T[:CUT], integrals.T[CUT:]
    near, far = swap_near(first), swap_far(first)
    near_next, far_next = swap_near(second), swap_far(second)
    swapped = swap_core(near_next), swap_core(far_next)
    low, high = shift_x(after(ahead[:4], *swapped), -1), shift_x(after(behind[4:], *swapped), 1)
    t = (here, ahead, low, high, behind, last)

    def exchange(v):
        return lax.all_to_all(
            v.reshape(-1, rows, v.shape[1]), ("x", "z"), split_axis=0, concat_axis=0, tiled=True
        )

    (result,) = product(spot, t, [[near], [swap_core(near)], [far], [swap_core(far)]])
    (result_next,) = product(
        spot, t, [[near_next], [swapped[0]], [far_next], [swapped[1]]]
    )
    other_block = [exchange(result), exchange(result_next)]
    across = [swap_far(near), swap_near(far_next)]
    own, own2, across2 = [first, second], [swap_core(first), swap_core(second)], [swap_core(v) for v in across]
    (own_block,) = product(spot, t, [own, own2, across, across2])
    own_block = exchange(after(own_block, other_block[1]))
    out = place((1 - yl).reshape(1), other_block)
    return place(yl.reshape(1), [own_block], out)


def solution(mesh):
    grid = Mesh(mesh.devices.reshape(2, 4, 8, 2, 2), AXES)
    return jax.shard_map(
        on_device,
        mesh=grid,
        in_specs=(P(AXES, None), P(("yh", "core"), ("yl", "x", "z"))),
        out_specs=P(AXES, None),
        check_vma=False,
    )
```
